32 devices in a mesh: ctx: 8 (over z, y), tp: 4 (over x, core).
Axes of the slice: x: 2, y: 2, z: 4, core: 2. Of those that a mesh axis runs over, the one named last changes fastest.
Arguments:
- features: bfloat16 [3, 1024, 4096], P(None, 'ctx', 'tp'), may hold values from -6 to 6
- out_grad: bfloat16 [1024, 4096], P('ctx', 'tp'), may hold values from -6 to 6
- attn_parts: bfloat16 [4, 1024, 4096], P('tp', 'ctx'), may hold values from -6 to 6
- short_filt: bfloat16 [3, 256, 7], P(None, 'tp'), may hold values from -2 to 2
- med_filt: bfloat16 [256, 128], P('tp'), may hold values from -0.5 to 0.5
- piece_home: int32 [32], replicated, may hold values from 0 to 7, as said below
- piece_start: int32 [32], replicated, may hold values from 0 to 96, as said below
Outputs:
- feat_grad: bfloat16 [3, 1024, 4096], P(None, 'ctx', 'tp')
- short_grad: float32 [3, 256, 7], P(None, 'tp')
- med_grad: float32 [256, 128], P('tp')
The draws below stay inside these ranges and needn't reach their ends.
Inputs may be any that keep to these rules, and one draw needn't show every extreme that they name: `piece_home`: entry i * 4 + l names the home device of the piece of 32 rows that starts at row l * 32 of device i in the balanced layout. With piece_start the entries name every piece of every home device exactly once, and no device of the balanced layout holds two pieces of the same home device. `piece_start`: A multiple of 32.
All inputs are finite; a program needn't handle non-finite values.
Results may differ from the reference program's by a relative error of at most 0.012.
Values may be sent and summed in bfloat16 or wider, within the bound.
A program may use at most 64 MiB of HBM per device.

```python
import math
import jax
import jax.numpy as jnp
from jax import lax

CH = 4096
GROUP = 16
SK = 7
MK = 128
TOK_DEV = 128
PIECES_DEV = 4
PIECE = 32
TOKENS = 1024
GROUPS = 256
N_CTX = 8
N_TP = 4


def route_tables(key):
    base = jax.random.fold_in(key, 7)
    keys = jax.random.split(base, 5)
    offsets = jax.random.permutation(keys[0], N_CTX)[:PIECES_DEV]
    outer = jax.random.permutation(keys[1], N_CTX)
    inner = jax.random.permutation(keys[2], N_CTX)
    local = jax.vmap(lambda one: jax.random.permutation(one, PIECES_DEV))(jax.random.split(keys[3], N_CTX))
    slots = jax.vmap(lambda one: jax.random.permutation(one, PIECES_DEV))(jax.random.split(keys[4], N_CTX))
    home = outer[(inner[:, None] + offsets[local]) % N_CTX]
    start = PIECE * slots[home, local]
    return (home.reshape(-1).astype(jnp.int32), start.reshape(-1).astype(jnp.int32))


def draw_piece_home(key, part):
    return route_tables(key)[0]


def draw_piece_start(key, part):
    return route_tables(key)[1]


def raised(array, key, source, target, blocks, factor):
    def block_of(dim):
        return (jnp.arange(array.shape[dim]) // (array.shape[dim] // blocks)).reshape((-1,) + (1,) * (array.ndim - 1 - dim))

    near = jax.random.permutation(key, blocks)[block_of(target)]
    far = (block_of(target) + blocks // 2) % blocks
    return jnp.where((block_of(source) == near) | (block_of(source) == far), factor * array, array)


def level_of(key, extent, pieces, smallest, high):
    def one(axis_at, parts):
        draws = jax.random.uniform(jax.random.fold_in(jax.random.fold_in(key, 6), axis_at), (parts,), jnp.float32, smallest / len(pieces), high / len(pieces))
        return jnp.repeat(jnp.exp(draws), extent[axis_at] // parts).reshape((-1,) + (1,) * (len(extent) - axis_at - 1))

    factor_of = one(*pieces[0])
    for cut in pieces[1:]:
        factor_of = factor_of * one(*cut)
    return factor_of


def bell_draw(key, shape, deviation, limit, shards=(), kind=jnp.bfloat16):
    result = deviation * jax.random.normal(key, shape, jnp.float32)
    if shards:
        result = result * level_of(key, shape, shards, -0.22, 0.18)
    return jnp.clip(result, -limit, limit).astype(kind)


def gaussian_with(stream_key, extent, scale, most, shards, heavy, kind=jnp.bfloat16):
    array = scale * jax.random.normal(stream_key, extent, jnp.float32)
    if shards:
        array = array * level_of(stream_key, extent, shards, -0.22, 0.18)
    return jnp.clip(raised(array, jax.random.fold_in(stream_key, 3), *heavy), -most, most).astype(kind)


def setup_inputs(seed: int = 0) -> dict:
    key_of = jax.random.split(jax.random.key(seed), 8)
    return {
        "features": bell_draw(key_of[0], (3, TOKENS, CH), 1.0, 6.0, ((1, 8), (2, 4))),
        "out_grad": bell_draw(key_of[1], (TOKENS, CH), 1.0, 6.0, ((0, 8), (1, 4))),
        "attn_parts": gaussian_with(key_of[2], (N_TP, TOKENS, CH), 0.5, 6.0, ((0, 4), (1, 8)), (0, 2, 4, 2.0)),
        "short_filt": bell_draw(key_of[3], (3, GROUPS, SK), SK ** -0.5, 2.0, ((1, 4),)),
        "med_filt": bell_draw(key_of[4], (GROUPS, MK), MK ** -0.5, 0.5, ((0, 4),)),
        "piece_home": draw_piece_home(jax.random.fold_in(key_of[7], 71), 0),
        "piece_start": draw_piece_start(jax.random.fold_in(key_of[7], 71), 0),
    }


def causal_table(filt):
    taps = filt.shape[1]
    lag = jnp.arange(taps, dtype=jnp.int32)[:, None] + taps - 1 - jnp.arange(2 * taps - 1, dtype=jnp.int32)[None, :]
    valid = (lag >= 0) & (lag < taps)
    return jnp.where(valid[None], filt[:, jnp.clip(lag, 0, taps - 1)], jnp.float32(0.0))

def anti_table(filt):
    taps = filt.shape[1]
    lag = jnp.arange(2 * taps - 1, dtype=jnp.int32)[None, :] - jnp.arange(taps, dtype=jnp.int32)[:, None]
    valid = (lag >= 0) & (lag < taps)
    return jnp.where(valid[None], filt[:, jnp.clip(lag, 0, taps - 1)], jnp.float32(0.0))

def band_apply(table, padded, rows):
    taps = table.shape[1]
    groups = table.shape[0]
    width = padded.shape[1]

    def one(block):
        window = lax.dynamic_slice_in_dim(padded, block * taps, 2 * taps - 1, 0).astype(jnp.float32)
        window = window.reshape(2 * taps - 1, groups, width // groups)
        return jnp.einsum('gtu,ugc->tgc', table, window).reshape(taps, width)
    return lax.map(one, jnp.arange(rows // taps, dtype=jnp.int32)).reshape(rows, width)

def lag_sums(grads, padded, rows, groups):
    taps = MK
    width = grads.shape[1]
    rowsel = jnp.arange(taps, dtype=jnp.int32)[:, None]
    colsel = rowsel + taps - 1 - jnp.arange(taps, dtype=jnp.int32)[None, :]

    def one(total, block):
        left = lax.dynamic_slice_in_dim(grads, block * taps, taps, 0).astype(jnp.float32).reshape(taps, groups, width // groups)
        window = lax.dynamic_slice_in_dim(padded, block * taps, 2 * taps - 1, 0).astype(jnp.float32)
        window = window.reshape(2 * taps - 1, groups, width // groups)
        cross = jnp.einsum('tgc,ugc->gtu', left, window)
        picked = cross[:, rowsel, colsel]
        return (total + lax.optimization_barrier(jnp.sum(picked, axis=1)), None)
    start = jnp.zeros((groups, taps), jnp.float32)
    total, _ = lax.scan(one, start, jnp.arange(rows // taps, dtype=jnp.int32))
    return total

def short_forward(stream, filt):
    weights = jnp.repeat(filt, GROUP, axis=0)
    padded = jnp.pad(stream.astype(jnp.float32), ((SK - 1, 0), (0, 0)))
    total = jnp.zeros((TOKENS, stream.shape[1]), jnp.float32)
    for lag in range(SK):
        total = total + weights[:, lag][None, :] * padded[SK - 1 - lag:SK - 1 - lag + TOKENS]
    return total

def short_backward(grads, filt):
    weights = jnp.repeat(filt, GROUP, axis=0)
    padded = jnp.pad(grads, ((0, SK - 1), (0, 0)))
    total = jnp.zeros_like(grads)
    for lag in range(SK):
        total = total + weights[:, lag][None, :] * padded[lag:lag + TOKENS]
    return total

def short_lags(grads, stream):
    padded = jnp.pad(stream.astype(jnp.float32), ((SK - 1, 0), (0, 0)))
    columns = []
    for lag in range(SK):
        summed = lax.optimization_barrier(jnp.sum(grads * padded[SK - 1 - lag:SK - 1 - lag + TOKENS], axis=0))
        columns.append(summed.reshape(-1, GROUP).sum(axis=1))
    return jnp.stack(columns, axis=1)

def reference(features, out_grad, attn_parts, short_filt, med_filt, piece_home, piece_start):
    attn_sum = lax.optimization_barrier(jnp.sum(attn_parts.astype(jnp.float32), axis=0)).astype(jnp.bfloat16)
    target = (piece_home * TOK_DEV + piece_start)[:, None] + jnp.arange(PIECE, dtype=jnp.int32)[None, :]
    attn_home = jnp.zeros_like(attn_sum).at[target.reshape(-1)].set(attn_sum)
    slab = CH // N_TP
    slab_groups = slab // GROUP
    factor = 1.0 / math.sqrt(TOKENS * GROUP)
    grads_out, shorts_out, meds_out = ([], [], [])
    for index in range(N_TP):
        low = index * slab
        stream_in = features[:, :, low:low + slab]
        filt_short = short_filt[:, index * slab_groups:(index + 1) * slab_groups, :].astype(jnp.float32)
        filt_med = med_filt[index * slab_groups:(index + 1) * slab_groups, :].astype(jnp.float32)
        grad = out_grad[:, low:low + slab].astype(jnp.float32) + attn_home[:, low:low + slab].astype(jnp.float32)
        query = short_forward(stream_in[0], filt_short[0])
        keys = short_forward(stream_in[1], filt_short[1])
        values = short_forward(stream_in[2], filt_short[2])
        keyval = (keys * values).astype(jnp.bfloat16)
        key_pad = jnp.pad(keyval, ((MK - 1, 0), (0, 0)))
        mixed = band_apply(causal_table(filt_med), key_pad, TOKENS)
        dquery = grad * mixed
        dmix = (grad * query).astype(jnp.bfloat16)
        dkeyval = band_apply(anti_table(filt_med), jnp.pad(dmix, ((0, MK - 1), (0, 0))), TOKENS)
        dstreams = [dquery, dkeyval * values, dkeyval * keys]
        grads_out.append(jnp.stack([short_backward(dstreams[s], filt_short[s]) for s in range(3)]).astype(jnp.bfloat16))
        shorts_out.append(jnp.stack([short_lags(dstreams[s], stream_in[s]) for s in range(3)]) * factor)
        meds_out.append(lag_sums(dmix, key_pad, TOKENS, slab_groups) * factor)
    return (jnp.concatenate(grads_out, axis=2), jnp.concatenate(shorts_out, axis=1), jnp.concatenate(meds_out, axis=0))
```

```python
import functools
import math

import jax
import jax.numpy as jnp
from jax import lax
from jax.experimental import pallas as pl
from jax.experimental.pallas import tpu as pltpu
from jax.sharding import PartitionSpec as P

GROUP = 16
MESH = pl.DeviceIdType.MESH
LANES = 256
EDGE = 8


def cost(flops, bytes_accessed):
    return pl.CostEstimate(flops=flops, bytes_accessed=bytes_accessed, transcendentals=0)


def plane(rows, axis):
    return lax.broadcasted_iota(jnp.int32, (rows, rows), axis)


def whole_kernel(
    n, tp, inline, factor,
    home_hbm, start_hbm, attn_hbm, feat_hbm, grad_hbm, taps_hbm, med_hbm,
    feat_out, short_out, med_out,
    home, start, feat_ref, out_grad_ref, mine_ref, taps_ref, med_ref,
    wt_ref, filt_ref, back_ref, member_ref, ext, short_ref,
    streams_ref, kv_ref, before_ref, dmix_ref, ds_ref, acc,
    got, passed, crossed, pieces, stage, landed, ready,
    rim_in, key_in, mix_in, head_ref, tail_in,
    flat_ref, part_ref, sums, gathered, last_ref, last_in, late_ref, late_in,
    local, pair_send, pair_recv, cross_send, cross_recv, send, recv, rim_sems, halo_send, halo_recv,
    send1, recv1, send2, recv2, send3, recv3, send4, recv4,
):
    me = lax.axis_index("ctx")
    col = lax.axis_index("tp")
    f32 = jnp.float32
    nc, rows, chunk = kv_ref.shape
    width = nc * chunk
    taps = taps_ref.shape[1]
    groups, long_taps = med_ref.shape
    per_device, piece_rows = pieces.shape[1:3]
    near = chunk // GROUP
    half = tp // 2
    side, row = lax.rem(col, 2), col // 2
    partner = row * 2 + 1 - side
    kind = kv_ref.dtype
    first = me == 0
    last = me == n - 1
    barrier = pltpu.get_barrier_semaphore()

    def other(d):
        return lax.rem(row + d, half) * 2 + side

    def peers(act):
        def step(k, carry):
            act(k)
            return carry

        lax.fori_loop(1, n, step, 0)

    def greet(k):
        pl.semaphore_signal(
            barrier, inc=1, device_id={"ctx": lax.rem(me + k, n)}, device_id_type=MESH
        )

    peers(greet)
    pl.semaphore_signal(barrier, inc=1, device_id={"tp": partner}, device_id_type=MESH)
    for d in range(1, half):
        pl.semaphore_signal(barrier, inc=1, device_id={"tp": other(d)}, device_id_type=MESH)

    def slab(which):
        return pl.ds(pl.multiple_of(which * width, width), width)

    def part(which, q):
        return pl.ds(pl.multiple_of(which * width + q * chunk, chunk), chunk)

    loads = [
        pltpu.make_async_copy(source, target, local.at[i])
        for i, (source, target) in enumerate(
            [
                (taps_hbm, taps_ref), (med_hbm, med_ref), (feat_hbm, feat_ref),
                (home_hbm, home), (start_hbm, start), (grad_hbm, out_grad_ref),
            ]
            + [
                (attn_hbm.at[:, slab(other(d))], mine_ref.at[d]) for d in range(half)
            ]
        )
    ]
    for load in loads:
        load.start()

    def hop(source, target, by, sends, recvs):
        return pltpu.make_async_remote_copy(
            source, target, sends, recvs,
            device_id={"ctx": lax.rem(me + by + n, n)}, device_id_type=MESH,
        )

    def key_hop(q):
        return hop(kv_ref.at[q], key_in.at[q], 1, halo_send.at[0, q], halo_recv.at[0, q])

    def mix_hop(q):
        return hop(dmix_ref.at[q], mix_in.at[q], -1, halo_send.at[1, q], halo_recv.at[1, q])

    def tail_hop(q):
        return hop(head_ref.at[q], tail_in.at[q], -1, halo_send.at[2, q], halo_recv.at[2, q])

    def pair(d, q):
        line = lax.rem(row + d, half)
        return pltpu.make_async_remote_copy(
            attn_hbm.at[:, part(line * 2 + 1 - side, q)], got.at[d, q],
            pair_send.at[d, q], pair_recv.at[d, q],
            device_id={"tp": partner}, device_id_type=MESH,
        )

    def cross(d, q):
        return pltpu.make_async_remote_copy(
            passed.at[d, q], crossed.at[d, q], cross_send.at[d, q], cross_recv.at[d, q],
            device_id={"tp": other(d)}, device_id_type=MESH,
        )

    def route(q, k):
        return pltpu.make_async_remote_copy(
            stage.at[q, k], landed.at[q, k], send.at[q, k], recv.at[q, k],
            device_id={"ctx": lax.rem(me + k, n)}, device_id_type=MESH,
        )

    def scatter(k):
        peer = lax.rem(me + k, n)
        return pltpu.make_async_remote_copy(
            part_ref.at[peer], sums.at[k], send1.at[k], recv1.at[k],
            device_id={"ctx": peer}, device_id_type=MESH,
        )

    def gather(k):
        return pltpu.make_async_remote_copy(
            gathered.at[me], gathered.at[me], send2.at[k], recv2.at[k],
            device_id={"ctx": lax.rem(me + k, n)}, device_id_type=MESH,
        )

    def share_last(k):
        return pltpu.make_async_remote_copy(
            last_ref, last_in.at[k], send3.at[k], recv3.at[k],
            device_id={"ctx": lax.rem(me + k, n)}, device_id_type=MESH,
        )

    def share_late(k):
        return pltpu.make_async_remote_copy(
            late_ref, late_in.at[k], send4.at[k], recv4.at[k],
            device_id={"ctx": lax.rem(me + k, n)}, device_id_type=MESH,
        )

    def columns(q):
        return pl.ds(pl.multiple_of(q * chunk, chunk), chunk)

    def chunks(low, high, act):
        def step(q, carry):
            act(q)
            return carry

        lax.fori_loop(low, high, step, 0)

    loads[0].wait()
    loads[1].wait()
    spread = jnp.where(
        lax.broadcasted_iota(jnp.int32, (groups, width), 0)
        == lax.broadcasted_iota(jnp.int32, (groups, width), 1) // GROUP,
        1.0,
        0.0,
    ).astype(kind)
    for s in range(3):
        wt_ref[s, 0:taps] = jnp.dot(taps_ref[s], spread, preferred_element_type=f32)
    t, s = plane(long_taps, 0), plane(long_taps, 1)
    turn = jnp.where((t + s == 0) | (t + s == long_taps), 1.0, 0.0).astype(kind)
    filt_ref[...] = jnp.dot(med_ref[...], turn, preferred_element_type=f32)
    back_ref[...] = med_ref[...].astype(f32)
    owned = lax.broadcasted_iota(jnp.int32, (width, long_taps), 0) // GROUP
    lane = lax.broadcasted_iota(jnp.int32, (width, long_taps), 1)
    member_ref[0] = jnp.where(owned == lane, 1.0, 0.0).astype(kind)
    member_ref[1] = jnp.where(owned + groups == lane, 1.0, 0.0).astype(kind)
    short_ref[...] = jnp.zeros_like(short_ref)
    last_ref[...] = jnp.zeros_like(last_ref)
    late_ref[...] = jnp.zeros_like(late_ref)
    loads[2].wait()

    def stream(k, cols, count):
        total = wt_ref[k, 0:1, cols] * ext[EDGE : EDGE + count]
        for lag in range(1, taps):
            total = total + wt_ref[k, lag : lag + 1, cols] * ext[EDGE - lag : EDGE - lag + count]
        return total

    def stream_step(q):
        cols = columns(q)
        found = []
        for k in range(3):
            ext[0:EDGE] = jnp.zeros((EDGE, chunk), f32)
            ext[EDGE : EDGE + rows] = feat_ref[k, :, cols].astype(f32)
            found.append(stream(k, cols, rows))
            streams_ref[k, :, cols] = found[k]
        kv_ref[q] = (found[1] * found[2]).astype(kind)

    chunks(0, nc, stream_step)
    pl.semaphore_wait(barrier, n - 1 + half)

    rim_hop = hop(
        feat_hbm.at[:, pl.ds(rows - EDGE, EDGE), :], rim_in, 1, rim_sems.at[0], rim_sems.at[1]
    )
    rim_hop.start()
    for d in [d for d in range(1, half)] + [0]:
        chunks(0, nc, lambda q, d=d: pair(d, q).start())

    for d in range(1, half):
        loads[6 + d].wait()

        def pass_on(q, d=d):
            pair(d, q).wait()
            passed[d, q] = (
                mine_ref[d, :, columns(q)].astype(f32) + got[d, q].astype(f32)
            ).astype(kind)
            cross(d, q).start()

        chunks(0, nc, pass_on)

    loads[3].wait()
    loads[4].wait()
    loads[6].wait()
    if inline:

        def pick(peer):
            slot = jnp.int32(0)
            for i in range(per_device):
                slot = jnp.where(home[me * per_device + i] == peer, i, slot)
            return slot

        def origin_of(slot):
            source = jnp.int32(0)
            for i in range(n * per_device):
                hit = (home[i] == me) & (start[i] == slot * piece_rows)
                source = jnp.where(hit, i // per_device, source)
            return source

        origins = [origin_of(slot) for slot in range(per_device)]
    else:

        def pick(peer):
            return home[peer]

        origins = [start[slot] for slot in range(per_device)]

    rim_hop.wait()

    def fill(k, cols, count):
        ext[0:EDGE] = jnp.where(first, 0.0, rim_in[k, :, cols].astype(f32))
        ext[EDGE : EDGE + count] = feat_ref[k, 0:count, cols].astype(f32)

    def send_step(q):
        cols = columns(q)
        found = []
        for k in range(3):
            fill(k, cols, GROUP)
            found.append(stream(k, cols, GROUP))
            streams_ref[k, 0:GROUP, cols] = found[k]
        kv_ref[q, 0:GROUP] = (found[1] * found[2]).astype(kind)
        key_hop(q).start()
        pair(0, q).wait()
        total = mine_ref[0, :, cols].astype(f32) + got[0, q].astype(f32)
        for d in range(1, half):
            cross(d, q).wait()
            total = total + crossed[d, q].astype(f32)
        for i in range(per_device):
            pieces[q, i] = total[i * piece_rows : (i + 1) * piece_rows]

        def launch(k):
            stage[q, k] = pieces[q, pick(lax.rem(me + k, n))].astype(kind)
            route(q, k).start()

        peers(launch)
        landed[q, 0] = pieces[q, pick(me)].astype(kind)

    chunks(0, nc, send_step)
    loads[5].wait()
    owner = lax.broadcasted_iota(jnp.int32, (long_taps, chunk), 1) // GROUP
    flip = jnp.where(t + s == long_taps - 1, 1.0, 0.0).astype(kind)

    def banded(lines, q, window, near_mask):
        total = jnp.zeros((long_taps, chunk), f32)
        for g in range(near):
            line = jnp.broadcast_to(lines[pl.ds(q * near + g, 1), :], (long_taps, long_taps))
            wheel = pltpu.roll(line, 0, 1, stride=1, stride_axis=0)
            table = jnp.concatenate(
                [jnp.where(near_mask, wheel, 0.0), jnp.where(near_mask, 0.0, wheel)], axis=1
            ).astype(kind)
            product = jnp.dot(table, window, preferred_element_type=f32)
            total = jnp.where(owner == g, product, total)
        return total

    def short_sums(k, q, value):
        cols = columns(q)
        fill(k, cols, rows)
        for lag in range(taps):
            short_ref[lag : lag + 1] = jnp.sum(
                value * ext[EDGE - lag : EDGE - lag + rows], axis=0, keepdims=True
            )
        exact = short_ref[...]
        high = exact.astype(kind)
        rest = exact - high.astype(f32)
        middle = rest.astype(kind)
        low = (rest - middle.astype(f32)).astype(kind)
        found = jnp.zeros((EDGE, long_taps), f32)
        for term in (high, middle, low):
            found = found + jnp.dot(
                term, member_ref[1 if k == 2 else 0, cols, :], preferred_element_type=f32
            )
        return found

    def receive(q, lines):
        cols = columns(q)
        peers(lambda k: route(q, k).wait())
        ready[...] = landed[q]
        for slot in range(per_device):
            at = lax.rem(me - origins[slot] + n, n)
            acc[slot * piece_rows : (slot + 1) * piece_rows] = ready[at].astype(f32)
        acc[...] = out_grad_ref[:, cols].astype(f32) + acc[...]
        dmix_ref[q] = (acc[...] * streams_ref[0, :, cols]).astype(kind)
        mix_hop(q).start()
        key_hop(q).wait()
        before_ref[...] = jnp.where(first, 0.0, key_in[q].astype(f32)).astype(kind)
        window = jnp.concatenate([before_ref[...], kv_ref[q]], axis=0)
        flipped = jnp.dot(flip, dmix_ref[q], preferred_element_type=f32)
        for g in range(near):
            left = jnp.where(owner == g, flipped, 0.0).astype(kind)
            both = lax.dot_general(
                left, window, (((1,), (1,)), ((), ())), preferred_element_type=f32
            )
            ring = jnp.where(s + t <= long_taps - 1, both[:, long_taps:], both[:, :long_taps])
            ring = pltpu.roll(ring, 0, 1, stride=1, stride_axis=0)
            lines(g, jnp.sum(ring, axis=0, keepdims=True))
        value = acc[...] * banded(filt_ref, q, window, s > t)
        ds_ref[0, :, cols] = value
        last_ref[near : near + EDGE] = last_ref[near : near + EDGE] + short_sums(0, q, value)

    def early(q):
        def lines(g, line):
            flat_ref[pl.ds(q * near + g, 1), :] = line

        receive(q, lines)

    def final_lines(g, line):
        last_ref[g : g + 1] = line

    def back_step(q):
        cols = columns(q)
        mix_hop(q).wait()
        after = jnp.where(last, 0.0, mix_in[q].astype(f32)).astype(kind)
        window = jnp.concatenate([dmix_ref[q], after], axis=0)
        total = banded(back_ref, q, window, s >= t)
        for k in (1, 2):
            value = total * streams_ref[3 - k, :, cols]
            ds_ref[k, :, cols] = value
            late_ref[...] = late_ref[...] + short_sums(k, q, value)
        head_ref[q] = ds_ref[:, 0:EDGE, cols].astype(kind)
        tail_hop(q).start()

    def feat_step(q):
        cols = columns(q)
        tail_hop(q).wait()
        for k in range(3):
            ext[0:rows] = ds_ref[k, :, cols]
            ext[rows:] = jnp.where(last, 0.0, tail_in[q, k].astype(f32))
            total = wt_ref[k, 0:1, cols] * ds_ref[k, :, cols]
            for lag in range(1, taps):
                total = total + wt_ref[k, lag : lag + 1, cols] * ext[lag : lag + rows]
            feat_out[k, :, cols] = total.astype(feat_out.dtype)

    share = part_ref.shape[1]
    used = (nc - 1) * near

    early(0)

    def both_steps(q):
        early(q)
        back_step(q - 1)

    chunks(1, nc - 1, both_steps)
    if n * share > used:
        flat_ref[used : n * share] = jnp.zeros((n * share - used, long_taps), f32)
    for k in range(n):
        part_ref[k] = flat_ref[k * share : (k + 1) * share]
    peers(lambda k: scatter(k).start())
    sums[0] = part_ref[me]
    receive(nc - 1, final_lines)
    peers(lambda k: share_last(k).start())
    peers(lambda k: scatter(k).wait())
    result = sums[0]
    for k in range(1, n):
        result = result + sums[k]
    gathered[me] = result
    peers(lambda k: gather(k).start())
    chunks(nc - 2, nc, back_step)
    peers(lambda k: share_late(k).start())
    chunks(0, nc, feat_step)
    peers(lambda k: gather(k).wait())
    for k in range(n):
        flat_ref[k * share : (k + 1) * share] = gathered[k]
    peers(lambda k: share_last(k).wait())
    total = last_ref[...]
    for k in range(1, n):
        total = total + last_in[k]
    flat_ref[used:groups] = total[0:near]
    mirror = jnp.where(t + s == long_taps - 1, 1.0, 0.0)
    med_out[...] = factor * jnp.dot(
        flat_ref[0:groups], mirror, precision=lax.Precision.HIGHEST, preferred_element_type=f32
    )
    peers(lambda k: share_late(k).wait())
    late = late_ref[...]
    for k in range(1, n):
        late = late + late_in[k]
    short_out[0] = factor * total[near : near + taps, :groups]
    short_out[1] = factor * late[:taps, :groups]
    short_out[2] = factor * late[:taps, groups : 2 * groups]


def store_kernel(feat_ref, short_ref, med_ref, feat_out, short_out, med_out, sems):
    copies = [
        pltpu.make_async_copy(source, target, sems.at[i])
        for i, (source, target) in enumerate(
            [(feat_ref, feat_out), (short_ref, short_out), (med_ref, med_out)]
        )
    ]
    for copy in copies:
        copy.start()
    for copy in copies:
        copy.wait()


def tables(piece_home, piece_start, ctx_count, per_device, piece_rows):
    own_index = lax.axis_index("ctx")
    everyone = piece_home.reshape(ctx_count, per_device)
    positions = (piece_start // piece_rows).reshape(ctx_count, per_device)
    local_home = lax.dynamic_slice_in_dim(everyone, own_index, 1, 0)[0]
    device_ids = jnp.arange(ctx_count, dtype=jnp.int32)
    slot_ids = jnp.arange(per_device, dtype=jnp.int32)
    matches = local_home[None, :] == device_ids[:, None]
    send_slot = jnp.sum(jnp.where(matches, slot_ids[None, :], 0), axis=1)
    keyed = jnp.where(everyone == own_index, positions, -1)
    hits = jnp.any(keyed[:, :, None] == slot_ids[None, None, :], axis=1)
    source_of = jnp.sum(jnp.where(hits, device_ids[:, None], 0), axis=0)
    return send_slot.astype(jnp.int32), source_of.astype(jnp.int32)


def shards(features, out_grad, attn_parts, short_filt, med_filt, piece_home, piece_start):
    rows, width = out_grad.shape
    groups, taps = med_filt.shape
    short_taps = short_filt.shape[2]
    ctx_count = lax.axis_size("ctx")
    tp_count = lax.axis_size("tp")
    per_device = ctx_count // 2
    piece_rows = rows // per_device
    factor = 1.0 / math.sqrt(rows * ctx_count * GROUP)
    chunk = LANES
    nc = width // chunk
    near = chunk // GROUP
    f32, half = jnp.float32, features.dtype
    inline = ctx_count * per_device <= 64
    if inline:
        home, start = piece_home, piece_start
    else:
        home, start = tables(piece_home, piece_start, ctx_count, per_device, piece_rows)

    vmem = pl.BlockSpec(memory_space=pltpu.VMEM)
    hbm = pl.BlockSpec(memory_space=pltpu.HBM)
    dma = pltpu.SemaphoreType.DMA
    share = -(-((nc - 1) * near) // ctx_count)
    parts = pltpu.VMEM((ctx_count, share, taps), f32)
    held = pltpu.VMEM((nc, rows, chunk), half)
    wide = pltpu.VMEM((3, rows, width), f32)
    crossing = pltpu.VMEM((tp_count // 2, nc, rows, chunk), half)
    routed = pltpu.VMEM((nc, ctx_count, piece_rows, chunk), half)
    heads = pltpu.VMEM((nc, 3, EDGE, chunk), half)
    flags = dma((tp_count // 2, nc))
    lanes = dma((nc, ctx_count))
    peers = dma((ctx_count,))
    outs = (
        jax.ShapeDtypeStruct((3, rows, width), half),
        jax.ShapeDtypeStruct((3, short_taps, groups), f32),
        jax.ShapeDtypeStruct((groups, taps), f32),
    )
    found = pl.pallas_call(
        functools.partial(whole_kernel, ctx_count, tp_count, inline, factor),
        in_specs=[hbm] * 7,
        out_specs=(vmem,) * 3,
        out_shape=outs,
        scratch_shapes=[
            pltpu.SMEM(home.shape, jnp.int32), pltpu.SMEM(start.shape, jnp.int32),
            pltpu.VMEM((3, rows, width), half), pltpu.VMEM((rows, width), half),
            pltpu.VMEM((tp_count // 2, rows, width), half),
            pltpu.VMEM((3, short_taps, groups), half), pltpu.VMEM((groups, taps), half),
            pltpu.VMEM((3, 8, width), f32), pltpu.VMEM((groups, taps), f32),
            pltpu.VMEM((groups, taps), f32), pltpu.VMEM((2, width, taps), half),
            pltpu.VMEM((rows + EDGE, chunk), f32), pltpu.VMEM((EDGE, chunk), f32),
            wide, held, pltpu.VMEM((rows, chunk), half), held, wide,
            pltpu.VMEM((rows, chunk), f32),
            crossing, crossing, crossing,
            pltpu.VMEM((nc, per_device, piece_rows, chunk), f32), routed, routed,
            pltpu.VMEM((ctx_count, piece_rows, chunk), half),
            pltpu.VMEM((3, EDGE, width), half), held, held, heads, heads,
            pltpu.VMEM((max(groups, ctx_count * share), taps), f32), parts, parts, parts,
            pltpu.VMEM((near + EDGE, taps), f32), pltpu.VMEM((ctx_count, near + EDGE, taps), f32),
            pltpu.VMEM((EDGE, taps), f32), pltpu.VMEM((ctx_count, EDGE, taps), f32),
            dma((6 + tp_count // 2,)), flags, flags, flags, flags, lanes, lanes,
            dma((2,)), dma((3, nc)), dma((3, nc)),
            peers, peers, peers, peers, peers, peers, peers, peers,
        ],
        compiler_params=pltpu.CompilerParams(
            collective_id=0, has_side_effects=True, vmem_limit_bytes=36 * 1024 * 1024
        ),
        cost_estimate=cost(12 * groups * taps * taps * chunk, 40 * rows * width),
    )(
        *[
            pltpu.with_memory_space_constraint(x, pltpu.HBM)
            for x in (
                home, start, attn_parts[0], features, out_grad,
                jnp.transpose(short_filt, (0, 2, 1)), med_filt,
            )
        ]
    )
    feat_grad, short_grad, med_grad = pl.pallas_call(
        store_kernel,
        in_specs=[vmem] * 3,
        out_specs=(hbm,) * 3,
        out_shape=outs,
        scratch_shapes=[dma((3,))],
        compiler_params=pltpu.CompilerParams(vmem_limit_bytes=4 * 1024 * 1024),
        cost_estimate=cost(0, 8 * rows * width),
    )(*found)
    return feat_grad, jnp.transpose(short_grad, (0, 2, 1)), med_grad


def solution(mesh):
    return jax.shard_map(
        shards,
        mesh=mesh,
        in_specs=(
            P(None, "ctx", "tp"),
            P("ctx", "tp"),
            P("tp", "ctx", None),
            P(None, "tp", None),
            P("tp", None),
            P(),
            P(),
        ),
        out_specs=(P(None, "ctx", "tp"), P(None, "tp", None), P("tp", None)),
        check_vma=False,
    )
```

```python
import functools
import math

import jax
import jax.numpy as jnp
from jax import lax
from jax.experimental import pallas as pl
from jax.experimental.pallas import tpu as pltpu
from jax.sharding import PartitionSpec as P

GROUP = 16
MESH = pl.DeviceIdType.MESH
LANES = 256
EDGE = 8


def cost(flops, bytes_accessed):
    return pl.CostEstimate(flops=flops, bytes_accessed=bytes_accessed, transcendentals=0)


def plane(rows, axis):
    return lax.broadcasted_iota(jnp.int32, (rows, rows), axis)


def whole_kernel(
    n, tp, inline, factor,
    home_hbm, start_hbm, attn_hbm, feat_hbm, grad_hbm, taps_hbm, med_hbm,
    feat_out, short_out, med_out,
    home, start, feat_ref, out_grad_ref, mine_ref, taps_ref, med_ref,
    wt_ref, filt_ref, back_ref, member_ref, ext, short_ref,
    streams_ref, kv_ref, dmix_ref, ds_ref, acc,
    got, passed, crossed, pieces, stage, landed, ready,
    rim_in, key_in, mix_in, head_ref, tail_in,
    flat_ref, part_ref, sums, gathered, last_ref, last_in, late_ref, late_in,
    local, pair_send, pair_recv, cross_send, cross_recv, send, recv, rim_sems, halo_send, halo_recv,
    send1, recv1, send2, recv2, send3, recv3, send4, recv4,
):
    me = lax.axis_index("ctx")
    col = lax.axis_index("tp")
    f32 = jnp.float32
    nc, rows, chunk = kv_ref.shape
    width = nc * chunk
    taps = taps_ref.shape[1]
    groups, long_taps = med_ref.shape
    per_device, piece_rows = pieces.shape[1:3]
    near = chunk // GROUP
    half = tp // 2
    side, row = lax.rem(col, 2), col // 2
    partner = row * 2 + 1 - side
    kind = kv_ref.dtype
    barrier = pltpu.get_barrier_semaphore()

    def other(d):
        return lax.rem(row + d, half) * 2 + side

    def peers(act):
        def step(k, carry):
            act(k)
            return carry

        lax.fori_loop(1, n, step, 0)

    def greet(k):
        pl.semaphore_signal(
            barrier, inc=1, device_id={"ctx": lax.rem(me + k, n)}, device_id_type=MESH
        )

    peers(greet)
    pl.semaphore_signal(barrier, inc=1, device_id={"tp": partner}, device_id_type=MESH)
    for d in range(1, half):
        pl.semaphore_signal(barrier, inc=1, device_id={"tp": other(d)}, device_id_type=MESH)

    def slab(which):
        return pl.ds(pl.multiple_of(which * width, width), width)

    def part(which, q):
        return pl.ds(pl.multiple_of(which * width + q * chunk, chunk), chunk)

    loads = [
        pltpu.make_async_copy(source, target, local.at[i])
        for i, (source, target) in enumerate(
            [
                (taps_hbm, taps_ref), (med_hbm, med_ref), (feat_hbm, feat_ref),
                (home_hbm, home), (start_hbm, start), (grad_hbm, out_grad_ref),
            ]
            + [
                (attn_hbm.at[:, slab(other(d))], mine_ref.at[d]) for d in range(half)
            ]
        )
    ]
    for load in loads:
        load.start()

    def hop(source, target, by, sends, recvs):
        return pltpu.make_async_remote_copy(
            source, target, sends, recvs,
            device_id={"ctx": lax.rem(me + by + n, n)}, device_id_type=MESH,
        )

    def up(copy, begin):
        if begin:
            pl.when(me < n - 1)(copy.start)
        else:
            pl.when(me < n - 1)(copy.wait_send)
            pl.when(me > 0)(copy.wait_recv)

    def down(copy, begin):
        if begin:
            pl.when(me > 0)(copy.start)
        else:
            pl.when(me > 0)(copy.wait_send)
            pl.when(me < n - 1)(copy.wait_recv)

    def key_hop(q):
        body = pl.ds(GROUP, rows - GROUP)
        return hop(
            kv_ref.at[q, body], key_in.at[q, body], 1, halo_send.at[0, q], halo_recv.at[0, q]
        )

    def key_rest(q):
        body = pl.ds(0, GROUP)
        return hop(
            kv_ref.at[q, body], key_in.at[q, body], 1, halo_send.at[3, q], halo_recv.at[3, q]
        )

    def mix_hop(q):
        return hop(dmix_ref.at[q], mix_in.at[q], -1, halo_send.at[1, q], halo_recv.at[1, q])

    def tail_hop(q):
        return hop(head_ref.at[q], tail_in.at[q], -1, halo_send.at[2, q], halo_recv.at[2, q])

    def pair(d, q):
        line = lax.rem(row + d, half)
        return pltpu.make_async_remote_copy(
            attn_hbm.at[:, part(line * 2 + 1 - side, q)], got.at[d, q],
            pair_send.at[d, q], pair_recv.at[d, q],
            device_id={"tp": partner}, device_id_type=MESH,
        )

    def cross(d, q):
        return pltpu.make_async_remote_copy(
            passed.at[d, q], crossed.at[d, q], cross_send.at[d, q], cross_recv.at[d, q],
            device_id={"tp": other(d)}, device_id_type=MESH,
        )

    def route(q, k):
        return pltpu.make_async_remote_copy(
            stage.at[q, k], landed.at[q, k], send.at[q, k], recv.at[q, k],
            device_id={"ctx": lax.rem(me + k, n)}, device_id_type=MESH,
        )

    def scatter(k):
        peer = lax.rem(me + k, n)
        return pltpu.make_async_remote_copy(
            part_ref.at[peer], sums.at[k], send1.at[k], recv1.at[k],
            device_id={"ctx": peer}, device_id_type=MESH,
        )

    def gather(k):
        return pltpu.make_async_remote_copy(
            gathered.at[me], gathered.at[me], send2.at[k], recv2.at[k],
            device_id={"ctx": lax.rem(me + k, n)}, device_id_type=MESH,
        )

    def share_last(k):
        return pltpu.make_async_remote_copy(
            last_ref, last_in.at[k], send3.at[k], recv3.at[k],
            device_id={"ctx": lax.rem(me + k, n)}, device_id_type=MESH,
        )

    def share_late(k):
        return pltpu.make_async_remote_copy(
            late_ref, late_in.at[k], send4.at[k], recv4.at[k],
            device_id={"ctx": lax.rem(me + k, n)}, device_id_type=MESH,
        )

    def columns(q):
        return pl.ds(pl.multiple_of(q * chunk, chunk), chunk)

    def chunks(low, high, act):
        def step(q, carry):
            act(q)
            return carry

        lax.fori_loop(low, high, step, 0)

    @pl.when(me == 0)
    def clear_first():
        rim_in[...] = jnp.zeros_like(rim_in)
        key_in[...] = jnp.zeros_like(key_in)

    @pl.when(me == n - 1)
    def clear_last():
        mix_in[...] = jnp.zeros_like(mix_in)
        tail_in[...] = jnp.zeros_like(tail_in)

    pl.semaphore_wait(barrier, n - 1 + half)
    rim_hop = hop(
        feat_hbm.at[:, pl.ds(rows - EDGE, EDGE), :], rim_in, 1, rim_sems.at[0], rim_sems.at[1]
    )
    up(rim_hop, True)
    for d in [d for d in range(1, half)] + [0]:
        chunks(0, nc, lambda q, d=d: pair(d, q).start())

    loads[0].wait()
    loads[1].wait()
    spread = jnp.where(
        lax.broadcasted_iota(jnp.int32, (groups, width), 0)
        == lax.broadcasted_iota(jnp.int32, (groups, width), 1) // GROUP,
        1.0,
        0.0,
    ).astype(kind)
    for s in range(3):
        wt_ref[s, 0:taps] = jnp.dot(taps_ref[s], spread, preferred_element_type=f32)
    loads[2].wait()

    def stream(k, cols, count):
        total = wt_ref[k, 0:1, cols] * ext[EDGE : EDGE + count]
        for lag in range(1, taps):
            total = total + wt_ref[k, lag : lag + 1, cols] * ext[EDGE - lag : EDGE - lag + count]
        return total

    def stream_step(q):
        cols = columns(q)
        found = []
        for k in range(3):
            ext[0:EDGE] = jnp.zeros((EDGE, chunk), f32)
            ext[EDGE : EDGE + rows] = feat_ref[k, :, cols].astype(f32)
            found.append(stream(k, cols, rows))
            streams_ref[k, :, cols] = found[k]
        kv_ref[q, GROUP:] = (found[1] * found[2])[GROUP:].astype(kind)
        up(key_hop(q), True)
        for d in range(1, half):
            pair(d, q).wait()
            passed[d, q] = (mine_ref[d, :, cols].astype(f32) + got[d, q].astype(f32)).astype(kind)
            cross(d, q).start()

    for d in range(1, half):
        loads[6 + d].wait()
    chunks(0, nc, stream_step)
    t, s = plane(long_taps, 0), plane(long_taps, 1)
    turn = jnp.where((t + s == 0) | (t + s == long_taps), 1.0, 0.0).astype(kind)
    filt_ref[...] = jnp.dot(med_ref[...], turn, preferred_element_type=f32)
    back_ref[...] = med_ref[...].astype(f32)
    loads[3].wait()
    loads[4].wait()
    loads[6].wait()
    if inline:

        def pick(peer):
            slot = jnp.int32(0)
            for i in range(per_device):
                slot = jnp.where(home[me * per_device + i] == peer, i, slot)
            return slot

        def origin_of(slot):
            source = jnp.int32(0)
            for i in range(n * per_device):
                hit = (home[i] == me) & (start[i] == slot * piece_rows)
                source = jnp.where(hit, i // per_device, source)
            return source

        origins = [origin_of(slot) for slot in range(per_device)]
    else:

        def pick(peer):
            return home[peer]

        origins = [start[slot] for slot in range(per_device)]

    up(rim_hop, False)

    def fill(k, cols, count):
        ext[0:EDGE] = rim_in[k, :, cols].astype(f32)
        ext[EDGE : EDGE + count] = feat_ref[k, 0:count, cols].astype(f32)

    def rim_step(q):
        cols = columns(q)
        found = []
        for k in range(3):
            fill(k, cols, GROUP)
            found.append(stream(k, cols, GROUP))
            streams_ref[k, 0:GROUP, cols] = found[k]
        kv_ref[q, 0:GROUP] = (found[1] * found[2]).astype(kind)
        up(key_rest(q), True)

    chunks(0, nc, rim_step)
    owner = lax.broadcasted_iota(jnp.int32, (long_taps, chunk), 1) // GROUP
    flip = jnp.where(t + s == long_taps - 1, 1.0, 0.0).astype(kind)

    def banded(lines, q, window, near_mask):
        total = jnp.zeros((long_taps, chunk), f32)
        for g in range(near):
            line = jnp.broadcast_to(lines[pl.ds(q * near + g, 1), :], (long_taps, long_taps))
            wheel = pltpu.roll(line, 0, 1, stride=1, stride_axis=0)
            table = jnp.concatenate(
                [jnp.where(near_mask, wheel, 0.0), jnp.where(near_mask, 0.0, wheel)], axis=1
            ).astype(kind)
            product = jnp.dot(table, window, preferred_element_type=f32)
            total = jnp.where(owner == g, product, total)
        return total

    def send_step(q):
        cols = columns(q)
        pair(0, q).wait()
        total = mine_ref[0, :, cols].astype(f32) + got[0, q].astype(f32)
        for d in range(1, half):
            cross(d, q).wait()
            total = total + crossed[d, q].astype(f32)
        for i in range(per_device):
            pieces[q, i] = total[i * piece_rows : (i + 1) * piece_rows]

        def launch(k):
            stage[q, k] = pieces[q, pick(lax.rem(me + k, n))].astype(kind)
            route(q, k).start()

        peers(launch)
        landed[q, 0] = pieces[q, pick(me)].astype(kind)

    def mixed_step(q):
        up(key_hop(q), False)
        up(key_rest(q), False)
        window = jnp.concatenate([key_in[q], kv_ref[q]], axis=0)
        ds_ref[0, :, columns(q)] = banded(filt_ref, q, window, s > t)

    chunks(0, nc, send_step)
    owned = lax.broadcasted_iota(jnp.int32, (width, long_taps), 0) // GROUP
    lane = lax.broadcasted_iota(jnp.int32, (width, long_taps), 1)
    member_ref[0] = jnp.where(owned == lane, 1.0, 0.0).astype(kind)
    member_ref[1] = jnp.where(owned + groups == lane, 1.0, 0.0).astype(kind)
    short_ref[...] = jnp.zeros_like(short_ref)
    last_ref[...] = jnp.zeros_like(last_ref)
    late_ref[...] = jnp.zeros_like(late_ref)
    loads[5].wait()
    mixed_step(0)
    mixed_step(1)

    def short_sums(k, q, value):
        cols = columns(q)
        fill(k, cols, rows)
        for lag in range(taps):
            short_ref[lag : lag + 1] = jnp.sum(
                value * ext[EDGE - lag : EDGE - lag + rows], axis=0, keepdims=True
            )
        exact = short_ref[...]
        high = exact.astype(kind)
        rest = exact - high.astype(f32)
        middle = rest.astype(kind)
        low = (rest - middle.astype(f32)).astype(kind)
        found = jnp.zeros((EDGE, long_taps), f32)
        for term in (high, middle, low):
            found = found + jnp.dot(
                term, member_ref[1 if k == 2 else 0, cols, :], preferred_element_type=f32
            )
        return found

    def receive(q, lines):
        cols = columns(q)
        peers(lambda k: route(q, k).wait())
        ready[...] = landed[q]
        for slot in range(per_device):
            at = lax.rem(me - origins[slot] + n, n)
            acc[slot * piece_rows : (slot + 1) * piece_rows] = ready[at].astype(f32)
        acc[...] = out_grad_ref[:, cols].astype(f32) + acc[...]
        dmix_ref[q] = (acc[...] * streams_ref[0, :, cols]).astype(kind)
        down(mix_hop(q), True)
        window = jnp.concatenate([key_in[q], kv_ref[q]], axis=0)
        flipped = jnp.dot(flip, dmix_ref[q], preferred_element_type=f32)
        for g in range(near):
            left = jnp.where(owner == g, flipped, 0.0).astype(kind)
            both = lax.dot_general(
                left, window, (((1,), (1,)), ((), ())), preferred_element_type=f32
            )
            ring = jnp.where(s + t <= long_taps - 1, both[:, long_taps:], both[:, :long_taps])
            ring = pltpu.roll(ring, 0, 1, stride=1, stride_axis=0)
            lines(g, jnp.sum(ring, axis=0, keepdims=True))
        value = acc[...] * ds_ref[0, :, cols]
        ds_ref[0, :, cols] = value
        last_ref[near : near + EDGE] = last_ref[near : near + EDGE] + short_sums(0, q, value)

    def early(q):
        def lines(g, line):
            flat_ref[pl.ds(q * near + g, 1), :] = line

        receive(q, lines)

    def final_lines(g, line):
        last_ref[g : g + 1] = line

    def back_step(q):
        cols = columns(q)
        down(mix_hop(q), False)
        window = jnp.concatenate([dmix_ref[q], mix_in[q]], axis=0)
        total = banded(back_ref, q, window, s >= t)
        for k in (1, 2):
            value = total * streams_ref[3 - k, :, cols]
            ds_ref[k, :, cols] = value
            late_ref[...] = late_ref[...] + short_sums(k, q, value)
        head_ref[q] = ds_ref[:, 0:EDGE, cols].astype(kind)
        down(tail_hop(q), True)

    def feat_rows(k, q, low, tail):
        cols = columns(q)
        count = rows - low
        ext[0:count] = ds_ref[k, low:, cols]
        ext[count : count + EDGE] = tail
        total = wt_ref[k, 0:1, cols] * ext[0:count]
        for lag in range(1, taps):
            total = total + wt_ref[k, lag : lag + 1, cols] * ext[lag : lag + count]
        feat_out[k, low:, cols] = total.astype(feat_out.dtype)

    def feat_step(q):
        for k in range(3):
            feat_rows(k, q, 0, jnp.zeros((EDGE, chunk), f32))

    def tail_step(q):
        down(tail_hop(q), False)
        for k in range(3):
            feat_rows(k, q, rows - GROUP, tail_in[q, k].astype(f32))

    share = part_ref.shape[1]
    used = (nc - 1) * near

    early(0)

    def both_steps(q):
        mixed_step(q + 1)
        early(q)
        back_step(q - 1)

    chunks(1, nc - 1, both_steps)
    if n * share > used:
        flat_ref[used : n * share] = jnp.zeros((n * share - used, long_taps), f32)
    for k in range(n):
        part_ref[k] = flat_ref[k * share : (k + 1) * share]
    peers(lambda k: scatter(k).start())
    sums[0] = part_ref[me]
    receive(nc - 1, final_lines)
    peers(lambda k: share_last(k).start())
    back_step(nc - 2)
    chunks(0, nc - 2, feat_step)
    peers(lambda k: scatter(k).wait())
    result = sums[0]
    for k in range(1, n):
        result = result + sums[k]
    gathered[me] = result
    peers(lambda k: gather(k).start())
    back_step(nc - 1)
    peers(lambda k: share_late(k).start())
    chunks(nc - 2, nc, feat_step)
    chunks(0, nc, tail_step)
    peers(lambda k: gather(k).wait())
    for k in range(n):
        flat_ref[k * share : (k + 1) * share] = gathered[k]
    peers(lambda k: share_last(k).wait())
    total = last_ref[...]
    for k in range(1, n):
        total = total + last_in[k]
    flat_ref[used:groups] = total[0:near]
    mirror = jnp.where(t + s == long_taps - 1, 1.0, 0.0)
    med_out[...] = factor * jnp.dot(
        flat_ref[0:groups], mirror, precision=lax.Precision.HIGHEST, preferred_element_type=f32
    )
    peers(lambda k: share_late(k).wait())
    late = late_ref[...]
    for k in range(1, n):
        late = late + late_in[k]
    short_out[0] = factor * total[near : near + taps, :groups]
    short_out[1] = factor * late[:taps, :groups]
    short_out[2] = factor * late[:taps, groups : 2 * groups]


def store_kernel(feat_ref, short_ref, med_ref, feat_out, short_out, med_out, sems):
    copies = [
        pltpu.make_async_copy(source, target, sems.at[i])
        for i, (source, target) in enumerate(
            [(feat_ref, feat_out), (short_ref, short_out), (med_ref, med_out)]
        )
    ]
    for copy in copies:
        copy.start()
    for copy in copies:
        copy.wait()


def tables(piece_home, piece_start, ctx_count, per_device, piece_rows):
    own_index = lax.axis_index("ctx")
    everyone = piece_home.reshape(ctx_count, per_device)
    positions = (piece_start // piece_rows).reshape(ctx_count, per_device)
    local_home = lax.dynamic_slice_in_dim(everyone, own_index, 1, 0)[0]
    device_ids = jnp.arange(ctx_count, dtype=jnp.int32)
    slot_ids = jnp.arange(per_device, dtype=jnp.int32)
    matches = local_home[None, :] == device_ids[:, None]
    send_slot = jnp.sum(jnp.where(matches, slot_ids[None, :], 0), axis=1)
    keyed = jnp.where(everyone == own_index, positions, -1)
    hits = jnp.any(keyed[:, :, None] == slot_ids[None, None, :], axis=1)
    source_of = jnp.sum(jnp.where(hits, device_ids[:, None], 0), axis=0)
    return send_slot.astype(jnp.int32), source_of.astype(jnp.int32)


def shards(features, out_grad, attn_parts, short_filt, med_filt, piece_home, piece_start):
    rows, width = out_grad.shape
    groups, taps = med_filt.shape
    short_taps = short_filt.shape[2]
    ctx_count = lax.axis_size("ctx")
    tp_count = lax.axis_size("tp")
    per_device = ctx_count // 2
    piece_rows = rows // per_device
    factor = 1.0 / math.sqrt(rows * ctx_count * GROUP)
    chunk = LANES
    nc = width // chunk
    near = chunk // GROUP
    f32, half = jnp.float32, features.dtype
    inline = ctx_count * per_device <= 64
    if inline:
        home, start = piece_home, piece_start
    else:
        home, start = tables(piece_home, piece_start, ctx_count, per_device, piece_rows)

    vmem = pl.BlockSpec(memory_space=pltpu.VMEM)
    hbm = pl.BlockSpec(memory_space=pltpu.HBM)
    dma = pltpu.SemaphoreType.DMA
    share = -(-((nc - 1) * near) // ctx_count)
    parts = pltpu.VMEM((ctx_count, share, taps), f32)
    held = pltpu.VMEM((nc, rows, chunk), half)
    wide = pltpu.VMEM((3, rows, width), f32)
    crossing = pltpu.VMEM((tp_count // 2, nc, rows, chunk), half)
    routed = pltpu.VMEM((nc, ctx_count, piece_rows, chunk), half)
    heads = pltpu.VMEM((nc, 3, EDGE, chunk), half)
    flags = dma((tp_count // 2, nc))
    lanes = dma((nc, ctx_count))
    peers = dma((ctx_count,))
    outs = (
        jax.ShapeDtypeStruct((3, rows, width), half),
        jax.ShapeDtypeStruct((3, short_taps, groups), f32),
        jax.ShapeDtypeStruct((groups, taps), f32),
    )
    found = pl.pallas_call(
        functools.partial(whole_kernel, ctx_count, tp_count, inline, factor),
        in_specs=[hbm] * 7,
        out_specs=(vmem,) * 3,
        out_shape=outs,
        scratch_shapes=[
            pltpu.SMEM(home.shape, jnp.int32), pltpu.SMEM(start.shape, jnp.int32),
            pltpu.VMEM((3, rows, width), half), pltpu.VMEM((rows, width), half),
            pltpu.VMEM((tp_count // 2, rows, width), half),
            pltpu.VMEM((3, short_taps, groups), half), pltpu.VMEM((groups, taps), half),
            pltpu.VMEM((3, 8, width), f32), pltpu.VMEM((groups, taps), f32),
            pltpu.VMEM((groups, taps), f32), pltpu.VMEM((2, width, taps), half),
            pltpu.VMEM((rows + EDGE, chunk), f32), pltpu.VMEM((EDGE, chunk), f32),
            wide, held, held, wide,
            pltpu.VMEM((rows, chunk), f32),
            crossing, crossing, crossing,
            pltpu.VMEM((nc, per_device, piece_rows, chunk), f32), routed, routed,
            pltpu.VMEM((ctx_count, piece_rows, chunk), half),
            pltpu.VMEM((3, EDGE, width), half), held, held, heads, heads,
            pltpu.VMEM((max(groups, ctx_count * share), taps), f32), parts, parts, parts,
            pltpu.VMEM((near + EDGE, taps), f32), pltpu.VMEM((ctx_count, near + EDGE, taps), f32),
            pltpu.VMEM((EDGE, taps), f32), pltpu.VMEM((ctx_count, EDGE, taps), f32),
            dma((6 + tp_count // 2,)), flags, flags, flags, flags, lanes, lanes,
            dma((2,)), dma((4, nc)), dma((4, nc)),
            peers, peers, peers, peers, peers, peers, peers, peers,
        ],
        compiler_params=pltpu.CompilerParams(
            collective_id=0, has_side_effects=True, vmem_limit_bytes=36 * 1024 * 1024
        ),
        cost_estimate=cost(12 * groups * taps * taps * chunk, 40 * rows * width),
    )(
        *[
            pltpu.with_memory_space_constraint(x, pltpu.HBM)
            for x in (
                home, start, attn_parts[0], features, out_grad,
                jnp.transpose(short_filt, (0, 2, 1)), med_filt,
            )
        ]
    )
    feat_grad, short_grad, med_grad = pl.pallas_call(
        store_kernel,
        in_specs=[vmem] * 3,
        out_specs=(hbm,) * 3,
        out_shape=outs,
        scratch_shapes=[dma((3,))],
        compiler_params=pltpu.CompilerParams(vmem_limit_bytes=4 * 1024 * 1024),
        cost_estimate=cost(0, 8 * rows * width),
    )(*found)
    return feat_grad, jnp.transpose(short_grad, (0, 2, 1)), med_grad


def solution(mesh):
    return jax.shard_map(
        shards,
        mesh=mesh,
        in_specs=(
            P(None, "ctx", "tp"),
            P("ctx", "tp"),
            P("tp", "ctx", None),
            P(None, "tp", None),
            P("tp", None),
            P(),
            P(),
        ),
        out_specs=(P(None, "ctx", "tp"), P(None, "tp", None), P("tp", None)),
        check_vma=False,
    )
```

```python
import functools
import math

import jax
import jax.numpy as jnp
from jax import lax
from jax.experimental import pallas as pl
from jax.experimental.pallas import tpu as pltpu
from jax.sharding import PartitionSpec as P

GROUP = 16
MESH = pl.DeviceIdType.MESH
LANES = 256
EDGE = 8


def cost(flops, bytes_accessed):
    return pl.CostEstimate(flops=flops, bytes_accessed=bytes_accessed, transcendentals=0)


def plane(rows, axis):
    return lax.broadcasted_iota(jnp.int32, (rows, rows), axis)


def whole_kernel(
    n, tp, inline, factor,
    home_hbm, start_hbm, attn_hbm, feat_hbm, grad_hbm, taps_hbm, med_hbm,
    feat_out, short_out, med_out,
    home, start, feat_ref, out_grad_ref, mine_ref, taps_ref, med_ref,
    wt_ref, filt_ref, back_ref, member_ref, ext, short_ref,
    streams_ref, kv_ref, dmix_ref, ds_ref, acc,
    got, passed, crossed, pieces, stage, landed, ready,
    rim_in, key_in, mix_in, head_ref, tail_in,
    flat_ref, part_ref, sums, gathered, last_ref, last_in, late_ref, late_in,
    local, pair_send, pair_recv, cross_send, cross_recv, send, recv, rim_sems, halo_send, halo_recv,
    send1, recv1, send2, recv2, send3, recv3, send4, recv4,
):
    me = lax.axis_index("ctx")
    col = lax.axis_index("tp")
    f32 = jnp.float32
    nc, rows, chunk = kv_ref.shape
    width = nc * chunk
    taps = taps_ref.shape[1]
    groups, long_taps = med_ref.shape
    per_device, piece_rows = pieces.shape[1:3]
    near = chunk // GROUP
    half = tp // 2
    side, row = lax.rem(col, 2), col // 2
    partner = row * 2 + 1 - side
    kind = kv_ref.dtype
    barrier = pltpu.get_barrier_semaphore()

    def other(d):
        return lax.rem(row + d, half) * 2 + side

    def peers(act):
        def step(k, carry):
            act(k)
            return carry

        lax.fori_loop(1, n, step, 0)

    def greet(k):
        pl.semaphore_signal(
            barrier, inc=1, device_id={"ctx": lax.rem(me + k, n)}, device_id_type=MESH
        )

    peers(greet)
    pl.semaphore_signal(barrier, inc=1, device_id={"tp": partner}, device_id_type=MESH)
    for d in range(1, half):
        pl.semaphore_signal(barrier, inc=1, device_id={"tp": other(d)}, device_id_type=MESH)

    def slab(which):
        return pl.ds(pl.multiple_of(which * width, width), width)

    def part(which, q):
        return pl.ds(pl.multiple_of(which * width + q * chunk, chunk), chunk)

    loads = [
        pltpu.make_async_copy(source, target, local.at[i])
        for i, (source, target) in enumerate(
            [
                (taps_hbm, taps_ref), (med_hbm, med_ref), (feat_hbm, feat_ref),
                (home_hbm, home), (start_hbm, start), (grad_hbm, out_grad_ref),
            ]
            + [
                (attn_hbm.at[:, slab(other(d))], mine_ref.at[d]) for d in range(half)
            ]
        )
    ]
    for load in loads:
        load.start()

    def hop(source, target, by, sends, recvs):
        return pltpu.make_async_remote_copy(
            source, target, sends, recvs,
            device_id={"ctx": lax.rem(me + by + n, n)}, device_id_type=MESH,
        )

    def up(copy, begin):
        if begin:
            pl.when(me < n - 1)(copy.start)
        else:
            pl.when(me < n - 1)(copy.wait_send)
            pl.when(me > 0)(copy.wait_recv)

    def down(copy, begin):
        if begin:
            pl.when(me > 0)(copy.start)
        else:
            pl.when(me > 0)(copy.wait_send)
            pl.when(me < n - 1)(copy.wait_recv)

    def key_hop(q):
        body = pl.ds(GROUP, rows - GROUP)
        return hop(
            kv_ref.at[q, body], key_in.at[q, body], 1, halo_send.at[0, q], halo_recv.at[0, q]
        )

    def key_rest(q):
        body = pl.ds(0, GROUP)
        return hop(
            kv_ref.at[q, body], key_in.at[q, body], 1, halo_send.at[3, q], halo_recv.at[3, q]
        )

    def mix_hop(q):
        return hop(dmix_ref.at[q], mix_in.at[q], -1, halo_send.at[1, q], halo_recv.at[1, q])

    def tail_hop(q):
        return hop(head_ref.at[q], tail_in.at[q], -1, halo_send.at[2, q], halo_recv.at[2, q])

    def pair(d, q):
        line = lax.rem(row + d, half)
        return pltpu.make_async_remote_copy(
            attn_hbm.at[:, part(line * 2 + 1 - side, q)], got.at[d, q],
            pair_send.at[d, q], pair_recv.at[d, q],
            device_id={"tp": partner}, device_id_type=MESH,
        )

    def cross(d, q):
        return pltpu.make_async_remote_copy(
            passed.at[d, q], crossed.at[d, q], cross_send.at[d, q], cross_recv.at[d, q],
            device_id={"tp": other(d)}, device_id_type=MESH,
        )

    def route(q, k):
        return pltpu.make_async_remote_copy(
            stage.at[q, k], landed.at[q, k], send.at[q, k], recv.at[q, k],
            device_id={"ctx": lax.rem(me + k, n)}, device_id_type=MESH,
        )

    def scatter(k):
        peer = lax.rem(me + k, n)
        return pltpu.make_async_remote_copy(
            part_ref.at[peer], sums.at[k], send1.at[k], recv1.at[k],
            device_id={"ctx": peer}, device_id_type=MESH,
        )

    def gather(k):
        return pltpu.make_async_remote_copy(
            gathered.at[me], gathered.at[me], send2.at[k], recv2.at[k],
            device_id={"ctx": lax.rem(me + k, n)}, device_id_type=MESH,
        )

    def share_last(k):
        return pltpu.make_async_remote_copy(
            last_ref, last_in.at[k], send3.at[k], recv3.at[k],
            device_id={"ctx": lax.rem(me + k, n)}, device_id_type=MESH,
        )

    def share_late(k):
        return pltpu.make_async_remote_copy(
            late_ref, late_in.at[k], send4.at[k], recv4.at[k],
            device_id={"ctx": lax.rem(me + k, n)}, device_id_type=MESH,
        )

    def columns(q):
        return pl.ds(pl.multiple_of(q * chunk, chunk), chunk)

    def chunks(low, high, act):
        def step(q, carry):
            act(q)
            return carry

        lax.fori_loop(low, high, step, 0)

    @pl.when(me == 0)
    def clear_first():
        rim_in[...] = jnp.zeros_like(rim_in)
        key_in[...] = jnp.zeros_like(key_in)

    @pl.when(me == n - 1)
    def clear_last():
        mix_in[...] = jnp.zeros_like(mix_in)
        tail_in[...] = jnp.zeros_like(tail_in)

    pl.semaphore_wait(barrier, n - 1 + half)
    rim_hop = hop(
        feat_hbm.at[:, pl.ds(rows - EDGE, EDGE), :], rim_in, 1, rim_sems.at[0], rim_sems.at[1]
    )
    up(rim_hop, True)
    for d in [d for d in range(1, half)] + [0]:
        chunks(0, nc, lambda q, d=d: pair(d, q).start())

    loads[0].wait()
    loads[1].wait()
    spread = jnp.where(
        lax.broadcasted_iota(jnp.int32, (groups, width), 0)
        == lax.broadcasted_iota(jnp.int32, (groups, width), 1) // GROUP,
        1.0,
        0.0,
    ).astype(kind)
    for s in range(3):
        wt_ref[s, 0:taps] = jnp.dot(taps_ref[s], spread, preferred_element_type=f32)
    loads[2].wait()

    def stream(k, cols, count):
        total = wt_ref[k, 0:1, cols] * ext[EDGE : EDGE + count]
        for lag in range(1, taps):
            total = total + wt_ref[k, lag : lag + 1, cols] * ext[EDGE - lag : EDGE - lag + count]
        return total

    def stream_step(q):
        cols = columns(q)
        found = []
        for k in range(3):
            ext[0:EDGE] = jnp.zeros((EDGE, chunk), f32)
            ext[EDGE : EDGE + rows] = feat_ref[k, :, cols].astype(f32)
            found.append(stream(k, cols, rows))
            streams_ref[k, :, cols] = found[k]
        kv_ref[q, GROUP:] = (found[1] * found[2])[GROUP:].astype(kind)
        up(key_hop(q), True)
        for d in range(1, half):
            pair(d, q).wait()
            passed[d, q] = (mine_ref[d, :, cols].astype(f32) + got[d, q].astype(f32)).astype(kind)
            cross(d, q).start()

    for d in range(1, half):
        loads[6 + d].wait()
    chunks(0, nc, stream_step)
    t, s = plane(long_taps, 0), plane(long_taps, 1)
    turn = jnp.where((t + s == 0) | (t + s == long_taps), 1.0, 0.0).astype(kind)
    filt_ref[...] = jnp.dot(med_ref[...], turn, preferred_element_type=f32)
    back_ref[...] = med_ref[...].astype(f32)
    loads[3].wait()
    loads[4].wait()
    loads[6].wait()
    if inline:

        def pick(peer):
            slot = jnp.int32(0)
            for i in range(per_device):
                slot = jnp.where(home[me * per_device + i] == peer, i, slot)
            return slot

        def origin_of(slot):
            source = jnp.int32(0)
            for i in range(n * per_device):
                hit = (home[i] == me) & (start[i] == slot * piece_rows)
                source = jnp.where(hit, i // per_device, source)
            return source

        origins = [origin_of(slot) for slot in range(per_device)]
    else:

        def pick(peer):
            return home[peer]

        origins = [start[slot] for slot in range(per_device)]

    up(rim_hop, False)

    def fill(k, cols, count):
        ext[0:EDGE] = rim_in[k, :, cols].astype(f32)
        ext[EDGE : EDGE + count] = feat_ref[k, 0:count, cols].astype(f32)

    def rim_step(q):
        cols = columns(q)
        found = []
        for k in range(3):
            fill(k, cols, GROUP)
            found.append(stream(k, cols, GROUP))
            streams_ref[k, 0:GROUP, cols] = found[k]
        kv_ref[q, 0:GROUP] = (found[1] * found[2]).astype(kind)
        up(key_rest(q), True)

    chunks(0, nc, rim_step)
    owner = lax.broadcasted_iota(jnp.int32, (long_taps, chunk), 1) // GROUP
    flip = jnp.where(t + s == long_taps - 1, 1.0, 0.0).astype(kind)

    def banded(lines, q, window, near_mask):
        total = jnp.zeros((long_taps, chunk), f32)
        for g in range(near):
            line = jnp.broadcast_to(lines[pl.ds(q * near + g, 1), :], (long_taps, long_taps))
            wheel = pltpu.roll(line, 0, 1, stride=1, stride_axis=0)
            table = jnp.concatenate(
                [jnp.where(near_mask, wheel, 0.0), jnp.where(near_mask, 0.0, wheel)], axis=1
            ).astype(kind)
            product = jnp.dot(table, window, preferred_element_type=f32)
            total = jnp.where(owner == g, product, total)
        return total

    def send_step(q):
        cols = columns(q)
        pair(0, q).wait()
        total = mine_ref[0, :, cols].astype(f32) + got[0, q].astype(f32)
        for d in range(1, half):
            cross(d, q).wait()
            total = total + crossed[d, q].astype(f32)
        for i in range(per_device):
            pieces[q, i] = total[i * piece_rows : (i + 1) * piece_rows]

        def launch(k):
            stage[q, k] = pieces[q, pick(lax.rem(me + k, n))].astype(kind)
            route(q, k).start()

        peers(lambda j: launch(n - j))
        landed[q, 0] = pieces[q, pick(me)].astype(kind)

    def mixed_step(q):
        up(key_hop(q), False)
        up(key_rest(q), False)
        window = jnp.concatenate([key_in[q], kv_ref[q]], axis=0)
        ds_ref[0, :, columns(q)] = banded(filt_ref, q, window, s > t)

    chunks(0, nc, send_step)
    owned = lax.broadcasted_iota(jnp.int32, (width, long_taps), 0) // GROUP
    lane = lax.broadcasted_iota(jnp.int32, (width, long_taps), 1)
    member_ref[0] = jnp.where(owned == lane, 1.0, 0.0).astype(kind)
    member_ref[1] = jnp.where(owned + groups == lane, 1.0, 0.0).astype(kind)
    short_ref[...] = jnp.zeros_like(short_ref)
    last_ref[...] = jnp.zeros_like(last_ref)
    late_ref[...] = jnp.zeros_like(late_ref)
    loads[5].wait()
    chunks(0, nc - 1, mixed_step)

    def short_sums(k, q, value):
        cols = columns(q)
        fill(k, cols, rows)
        for lag in range(taps):
            short_ref[lag : lag + 1] = jnp.sum(
                value * ext[EDGE - lag : EDGE - lag + rows], axis=0, keepdims=True
            )
        exact = short_ref[...]
        high = exact.astype(kind)
        rest = exact - high.astype(f32)
        middle = rest.astype(kind)
        low = (rest - middle.astype(f32)).astype(kind)
        found = jnp.zeros((EDGE, long_taps), f32)
        for term in (high, middle, low):
            found = found + jnp.dot(
                term, member_ref[1 if k == 2 else 0, cols, :], preferred_element_type=f32
            )
        return found

    def receive(q):
        cols = columns(q)
        peers(lambda k: route(q, k).wait())
        ready[...] = landed[q]
        for slot in range(per_device):
            at = lax.rem(me - origins[slot] + n, n)
            acc[slot * piece_rows : (slot + 1) * piece_rows] = ready[at].astype(f32)
        acc[...] = out_grad_ref[:, cols].astype(f32) + acc[...]
        dmix_ref[q] = (acc[...] * streams_ref[0, :, cols]).astype(kind)
        down(mix_hop(q), True)

    def lag_step(q, lines):
        cols = columns(q)
        window = jnp.concatenate([key_in[q], kv_ref[q]], axis=0)
        flipped = jnp.dot(flip, dmix_ref[q], preferred_element_type=f32)
        for g in range(near):
            left = jnp.where(owner == g, flipped, 0.0).astype(kind)
            both = lax.dot_general(
                left, window, (((1,), (1,)), ((), ())), preferred_element_type=f32
            )
            ring = jnp.where(s + t <= long_taps - 1, both[:, long_taps:], both[:, :long_taps])
            ring = pltpu.roll(ring, 0, 1, stride=1, stride_axis=0)
            lines(g, jnp.sum(ring, axis=0, keepdims=True))
        value = acc[...] * ds_ref[0, :, cols]
        ds_ref[0, :, cols] = value
        last_ref[near : near + EDGE] = last_ref[near : near + EDGE] + short_sums(0, q, value)

    def early_lags(q):
        def lines(g, line):
            flat_ref[pl.ds(q * near + g, 1), :] = line

        lag_step(q, lines)

    def final_lines(g, line):
        last_ref[g : g + 1] = line

    def back_step(q):
        cols = columns(q)
        down(mix_hop(q), False)
        window = jnp.concatenate([dmix_ref[q], mix_in[q]], axis=0)
        total = banded(back_ref, q, window, s >= t)
        for k in (1, 2):
            value = total * streams_ref[3 - k, :, cols]
            ds_ref[k, :, cols] = value
            late_ref[...] = late_ref[...] + short_sums(k, q, value)
        head_ref[q] = ds_ref[:, 0:EDGE, cols].astype(kind)
        down(tail_hop(q), True)

    def feat_rows(k, q, low, tail):
        cols = columns(q)
        count = rows - low
        ext[0:count] = ds_ref[k, low:, cols]
        ext[count : count + EDGE] = tail
        total = wt_ref[k, 0:1, cols] * ext[0:count]
        for lag in range(1, taps):
            total = total + wt_ref[k, lag : lag + 1, cols] * ext[lag : lag + count]
        feat_out[k, low:, cols] = total.astype(feat_out.dtype)

    def feat_step(q):
        for k in range(3):
            feat_rows(k, q, 0, jnp.zeros((EDGE, chunk), f32))

    def tail_step(q):
        down(tail_hop(q), False)
        for k in range(3):
            feat_rows(k, q, rows - GROUP, tail_in[q, k].astype(f32))

    share = part_ref.shape[1]
    used = (nc - 1) * near

    receive(0)
    early_lags(0)
    receive(1)
    mixed_step(nc - 1)
    early_lags(1)

    def both_steps(q):
        receive(q)
        back_step(q - 2)
        early_lags(q)

    chunks(2, nc - 1, both_steps)
    if n * share > used:
        flat_ref[used : n * share] = jnp.zeros((n * share - used, long_taps), f32)
    for k in range(n):
        part_ref[k] = flat_ref[k * share : (k + 1) * share]
    peers(lambda k: scatter(k).start())
    sums[0] = part_ref[me]
    receive(nc - 1)
    back_step(nc - 3)
    lag_step(nc - 1, final_lines)
    peers(lambda k: share_last(k).start())
    back_step(nc - 2)
    feat_step(0)
    peers(lambda k: scatter(k).wait())
    result = sums[0]
    for k in range(1, n):
        result = result + sums[k]
    gathered[me] = result
    peers(lambda k: gather(k).start())
    back_step(nc - 1)
    peers(lambda k: share_late(k).start())
    chunks(1, nc, feat_step)
    chunks(0, nc, tail_step)
    peers(lambda k: gather(k).wait())
    for k in range(n):
        flat_ref[k * share : (k + 1) * share] = gathered[k]
    peers(lambda k: share_last(k).wait())
    total = last_ref[...]
    for k in range(1, n):
        total = total + last_in[k]
    flat_ref[used:groups] = total[0:near]
    mirror = jnp.where(t + s == long_taps - 1, 1.0, 0.0)
    med_out[...] = factor * jnp.dot(
        flat_ref[0:groups], mirror, precision=lax.Precision.HIGHEST, preferred_element_type=f32
    )
    peers(lambda k: share_late(k).wait())
    late = late_ref[...]
    for k in range(1, n):
        late = late + late_in[k]
    short_out[0] = factor * total[near : near + taps, :groups]
    short_out[1] = factor * late[:taps, :groups]
    short_out[2] = factor * late[:taps, groups : 2 * groups]


def store_kernel(feat_ref, short_ref, med_ref, feat_out, short_out, med_out, sems):
    copies = [
        pltpu.make_async_copy(source, target, sems.at[i])
        for i, (source, target) in enumerate(
            [(feat_ref, feat_out), (short_ref, short_out), (med_ref, med_out)]
        )
    ]
    for copy in copies:
        copy.start()
    for copy in copies:
        copy.wait()


def tables(piece_home, piece_start, ctx_count, per_device, piece_rows):
    own_index = lax.axis_index("ctx")
    everyone = piece_home.reshape(ctx_count, per_device)
    positions = (piece_start // piece_rows).reshape(ctx_count, per_device)
    local_home = lax.dynamic_slice_in_dim(everyone, own_index, 1, 0)[0]
    device_ids = jnp.arange(ctx_count, dtype=jnp.int32)
    slot_ids = jnp.arange(per_device, dtype=jnp.int32)
    matches = local_home[None, :] == device_ids[:, None]
    send_slot = jnp.sum(jnp.where(matches, slot_ids[None, :], 0), axis=1)
    keyed = jnp.where(everyone == own_index, positions, -1)
    hits = jnp.any(keyed[:, :, None] == slot_ids[None, None, :], axis=1)
    source_of = jnp.sum(jnp.where(hits, device_ids[:, None], 0), axis=0)
    return send_slot.astype(jnp.int32), source_of.astype(jnp.int32)


def shards(features, out_grad, attn_parts, short_filt, med_filt, piece_home, piece_start):
    rows, width = out_grad.shape
    groups, taps = med_filt.shape
    short_taps = short_filt.shape[2]
    ctx_count = lax.axis_size("ctx")
    tp_count = lax.axis_size("tp")
    per_device = ctx_count // 2
    piece_rows = rows // per_device
    factor = 1.0 / math.sqrt(rows * ctx_count * GROUP)
    chunk = LANES
    nc = width // chunk
    near = chunk // GROUP
    f32, half = jnp.float32, features.dtype
    inline = ctx_count * per_device <= 64
    if inline:
        home, start = piece_home, piece_start
    else:
        home, start = tables(piece_home, piece_start, ctx_count, per_device, piece_rows)

    vmem = pl.BlockSpec(memory_space=pltpu.VMEM)
    hbm = pl.BlockSpec(memory_space=pltpu.HBM)
    dma = pltpu.SemaphoreType.DMA
    share = -(-((nc - 1) * near) // ctx_count)
    parts = pltpu.VMEM((ctx_count, share, taps), f32)
    held = pltpu.VMEM((nc, rows, chunk), half)
    wide = pltpu.VMEM((3, rows, width), f32)
    crossing = pltpu.VMEM((tp_count // 2, nc, rows, chunk), half)
    routed = pltpu.VMEM((nc, ctx_count, piece_rows, chunk), half)
    heads = pltpu.VMEM((nc, 3, EDGE, chunk), half)
    flags = dma((tp_count // 2, nc))
    lanes = dma((nc, ctx_count))
    peers = dma((ctx_count,))
    outs = (
        jax.ShapeDtypeStruct((3, rows, width), half),
        jax.ShapeDtypeStruct((3, short_taps, groups), f32),
        jax.ShapeDtypeStruct((groups, taps), f32),
    )
    found = pl.pallas_call(
        functools.partial(whole_kernel, ctx_count, tp_count, inline, factor),
        in_specs=[hbm] * 7,
        out_specs=(vmem,) * 3,
        out_shape=outs,
        scratch_shapes=[
            pltpu.SMEM(home.shape, jnp.int32), pltpu.SMEM(start.shape, jnp.int32),
            pltpu.VMEM((3, rows, width), half), pltpu.VMEM((rows, width), half),
            pltpu.VMEM((tp_count // 2, rows, width), half),
            pltpu.VMEM((3, short_taps, groups), half), pltpu.VMEM((groups, taps), half),
            pltpu.VMEM((3, 8, width), f32), pltpu.VMEM((groups, taps), f32),
            pltpu.VMEM((groups, taps), f32), pltpu.VMEM((2, width, taps), half),
            pltpu.VMEM((rows + EDGE, chunk), f32), pltpu.VMEM((EDGE, chunk), f32),
            wide, held, held, wide,
            pltpu.VMEM((rows, chunk), f32),
            crossing, crossing, crossing,
            pltpu.VMEM((nc, per_device, piece_rows, chunk), f32), routed, routed,
            pltpu.VMEM((ctx_count, piece_rows, chunk), half),
            pltpu.VMEM((3, EDGE, width), half), held, held, heads, heads,
            pltpu.VMEM((max(groups, ctx_count * share), taps), f32), parts, parts, parts,
            pltpu.VMEM((near + EDGE, taps), f32), pltpu.VMEM((ctx_count, near + EDGE, taps), f32),
            pltpu.VMEM((EDGE, taps), f32), pltpu.VMEM((ctx_count, EDGE, taps), f32),
            dma((6 + tp_count // 2,)), flags, flags, flags, flags, lanes, lanes,
            dma((2,)), dma((4, nc)), dma((4, nc)),
            peers, peers, peers, peers, peers, peers, peers, peers,
        ],
        compiler_params=pltpu.CompilerParams(
            collective_id=0, has_side_effects=True, vmem_limit_bytes=36 * 1024 * 1024
        ),
        cost_estimate=cost(12 * groups * taps * taps * chunk, 40 * rows * width),
    )(
        *[
            pltpu.with_memory_space_constraint(x, pltpu.HBM)
            for x in (
                home, start, attn_parts[0], features, out_grad,
                jnp.transpose(short_filt, (0, 2, 1)), med_filt,
            )
        ]
    )
    feat_grad, short_grad, med_grad = pl.pallas_call(
        store_kernel,
        in_specs=[vmem] * 3,
        out_specs=(hbm,) * 3,
        out_shape=outs,
        scratch_shapes=[dma((3,))],
        compiler_params=pltpu.CompilerParams(vmem_limit_bytes=4 * 1024 * 1024),
        cost_estimate=cost(0, 8 * rows * width),
    )(*found)
    return feat_grad, jnp.transpose(short_grad, (0, 2, 1)), med_grad


def solution(mesh):
    return jax.shard_map(
        shards,
        mesh=mesh,
        in_specs=(
            P(None, "ctx", "tp"),
            P("ctx", "tp"),
            P("tp", "ctx", None),
            P(None, "tp", None),
            P("tp", None),
            P(),
            P(),
        ),
        out_specs=(P(None, "ctx", "tp"), P(None, "tp", None), P("tp", None)),
        check_vma=False,
    )
```

```python
import functools
import math

import jax
import jax.numpy as jnp
from jax import lax
from jax.experimental import pallas as pl
from jax.experimental.pallas import tpu as pltpu
from jax.sharding import PartitionSpec as P

GROUP = 16
MESH = pl.DeviceIdType.MESH
LANES = 256
EDGE = 8


def cost(flops, bytes_accessed):
    return pl.CostEstimate(flops=flops, bytes_accessed=bytes_accessed, transcendentals=0)


def plane(rows, axis):
    return lax.broadcasted_iota(jnp.int32, (rows, rows), axis)


def whole_kernel(
    n, tp, inline, factor,
    home_hbm, start_hbm, attn_hbm, feat_hbm, grad_hbm, taps_hbm, med_hbm,
    feat_out, short_out, med_out,
    home, start, feat_ref, out_grad_ref, mine_ref, taps_ref, med_ref,
    wt_ref, filt_ref, back_ref, member_ref, wide_ref, short_ref,
    streams_ref, kv_ref, dmix_ref, ds_ref, acc,
    got, passed, crossed, pieces, stage, landed, ready,
    rim_in, key_in, mix_in, head_ref, tail_in,
    flat_ref, part_ref, sums, gathered, last_ref, last_in, late_ref, late_in,
    local, pair_send, pair_recv, cross_send, cross_recv, send, recv, rim_sems, halo_send, halo_recv,
    send1, recv1, send2, recv2, send3, recv3, send4, recv4,
):
    me = lax.axis_index("ctx")
    col = lax.axis_index("tp")
    f32 = jnp.float32
    nc, rows, chunk = kv_ref.shape
    width = nc * chunk
    taps = taps_ref.shape[1]
    groups, long_taps = med_ref.shape
    per_device, piece_rows = pieces.shape[1:3]
    near = chunk // GROUP
    half = tp // 2
    side, row = lax.rem(col, 2), col // 2
    partner = row * 2 + 1 - side
    kind = kv_ref.dtype
    barrier = pltpu.get_barrier_semaphore()

    def other(d):
        return lax.rem(row + d, half) * 2 + side

    def peers(act):
        def step(k, carry):
            act(k)
            return carry

        lax.fori_loop(1, n, step, 0, unroll=inline)

    def greet(k):
        pl.semaphore_signal(
            barrier, inc=1, device_id={"ctx": lax.rem(me + k, n)}, device_id_type=MESH
        )

    peers(greet)
    pl.semaphore_signal(barrier, inc=1, device_id={"tp": partner}, device_id_type=MESH)
    for d in range(1, half):
        pl.semaphore_signal(barrier, inc=1, device_id={"tp": other(d)}, device_id_type=MESH)

    def slab(which):
        return pl.ds(pl.multiple_of(which * width, width), width)

    def part(which, q):
        return pl.ds(pl.multiple_of(which * width + q * chunk, chunk), chunk)

    def load(source, target, at):
        return pltpu.make_async_copy(source, target, local.at[at])

    loads = [
        load(taps_hbm, taps_ref, 0), load(med_hbm, med_ref, 1), load(feat_hbm, feat_ref, 2),
        load(home_hbm, home, 3), load(start_hbm, start, 4), load(grad_hbm, out_grad_ref, 5),
    ] + [
        load(attn_hbm.at[:, slab(other(d))], mine_ref.at[d], 6 + d) for d in range(half)
    ]
    for at in [6 + d for d in range(1, half)] + [0, 2]:
        loads[at].start()

    def hop(source, target, by, sends, recvs):
        return pltpu.make_async_remote_copy(
            source, target, sends, recvs,
            device_id={"ctx": lax.rem(me + by + n, n)}, device_id_type=MESH,
        )

    def up(copy, begin):
        if begin:
            pl.when(me < n - 1)(copy.start)
        else:
            pl.when(me < n - 1)(copy.wait_send)
            pl.when(me > 0)(copy.wait_recv)

    def down(copy, begin):
        if begin:
            pl.when(me > 0)(copy.start)
        else:
            pl.when(me > 0)(copy.wait_send)
            pl.when(me < n - 1)(copy.wait_recv)

    def key_hop(q):
        body = pl.ds(GROUP, rows - GROUP)
        return hop(
            kv_ref.at[q, body], key_in.at[q, body], 1, halo_send.at[0, q], halo_recv.at[0, q]
        )

    def key_rest(q):
        body = pl.ds(0, GROUP)
        return hop(
            kv_ref.at[q, body], key_in.at[q, body], 1, halo_send.at[3, q], halo_recv.at[3, q]
        )

    def mix_hop(q):
        return hop(dmix_ref.at[q], mix_in.at[q], -1, halo_send.at[1, q], halo_recv.at[1, q])

    def tail_hop(q):
        return hop(head_ref.at[q], tail_in.at[q], -1, halo_send.at[2, q], halo_recv.at[2, q])

    def pair(d, q):
        line = lax.rem(row + d, half)
        return pltpu.make_async_remote_copy(
            attn_hbm.at[:, part(line * 2 + 1 - side, q)], got.at[d, q],
            pair_send.at[d, q], pair_recv.at[d, q],
            device_id={"tp": partner}, device_id_type=MESH,
        )

    def cross(d, q):
        return pltpu.make_async_remote_copy(
            passed.at[d, q], crossed.at[d, q], cross_send.at[d, q], cross_recv.at[d, q],
            device_id={"tp": other(d)}, device_id_type=MESH,
        )

    def route(q, k):
        return pltpu.make_async_remote_copy(
            stage.at[q, k], landed.at[q, k], send.at[q, k], recv.at[q, k],
            device_id={"ctx": lax.rem(me + k, n)}, device_id_type=MESH,
        )

    def scatter(k):
        peer = lax.rem(me + k, n)
        return pltpu.make_async_remote_copy(
            part_ref.at[peer], sums.at[k], send1.at[k], recv1.at[k],
            device_id={"ctx": peer}, device_id_type=MESH,
        )

    def gather(k):
        return pltpu.make_async_remote_copy(
            gathered.at[me], gathered.at[me], send2.at[k], recv2.at[k],
            device_id={"ctx": lax.rem(me + k, n)}, device_id_type=MESH,
        )

    def share_last(k):
        return pltpu.make_async_remote_copy(
            last_ref, last_in.at[k], send3.at[k], recv3.at[k],
            device_id={"ctx": lax.rem(me + k, n)}, device_id_type=MESH,
        )

    def share_late(k):
        return pltpu.make_async_remote_copy(
            late_ref, late_in.at[k], send4.at[k], recv4.at[k],
            device_id={"ctx": lax.rem(me + k, n)}, device_id_type=MESH,
        )

    def columns(q):
        return pl.ds(pl.multiple_of(q * chunk, chunk), chunk)

    def chunks(low, high, act):
        def step(q, carry):
            act(q)
            return carry

        lax.fori_loop(low, high, step, 0)

    @pl.when(me == 0)
    def clear_first():
        rim_in[...] = jnp.zeros_like(rim_in)
        key_in[...] = jnp.zeros_like(key_in)

    @pl.when(me == n - 1)
    def clear_last():
        mix_in[...] = jnp.zeros_like(mix_in)
        tail_in[...] = jnp.zeros_like(tail_in)

    pl.semaphore_wait(barrier, n - 1 + half)
    rim_hop = hop(
        feat_hbm.at[:, pl.ds(rows - EDGE, EDGE), :], rim_in, 1, rim_sems.at[0], rim_sems.at[1]
    )
    up(rim_hop, True)
    for d in [d for d in range(1, half)] + [0]:
        chunks(0, nc, lambda q, d=d: pair(d, q).start())
    for at in (1, 6, 3, 4, 5):
        loads[at].start()

    wide_ref[:, 0:EDGE] = jnp.zeros((3, EDGE, width), f32)
    loads[0].wait()
    spread = jnp.where(
        lax.broadcasted_iota(jnp.int32, (groups, width), 0)
        == lax.broadcasted_iota(jnp.int32, (groups, width), 1) // GROUP,
        1.0,
        0.0,
    ).astype(kind)
    for s in range(3):
        wt_ref[s, 0:taps] = jnp.dot(taps_ref[s], spread, preferred_element_type=f32)
    loads[2].wait()

    def stream(k, cols, count):
        total = wt_ref[k, 0:1, cols] * wide_ref[k, EDGE : EDGE + count, cols]
        for lag in range(1, taps):
            rows_back = wide_ref[k, EDGE - lag : EDGE - lag + count, cols]
            total = total + wt_ref[k, lag : lag + 1, cols] * rows_back
        return total

    def stream_step(q):
        cols = columns(q)
        found = []
        for k in range(3):
            wide_ref[k, EDGE : EDGE + rows, cols] = feat_ref[k, :, cols].astype(f32)
            found.append(stream(k, cols, rows))
            streams_ref[k, :, cols] = found[k]
        kv_ref[q, GROUP:] = (found[1] * found[2])[GROUP:].astype(kind)
        up(key_hop(q), True)
        for d in range(1, half):
            pair(d, q).wait()
            passed[d, q] = (mine_ref[d, :, cols].astype(f32) + got[d, q].astype(f32)).astype(kind)
            cross(d, q).start()

    for d in range(1, half):
        loads[6 + d].wait()
    chunks(0, nc, stream_step)
    t, s = plane(long_taps, 0), plane(long_taps, 1)
    loads[1].wait()
    turn = jnp.where((t + s == 0) | (t + s == long_taps), 1.0, 0.0).astype(kind)
    filt_ref[...] = jnp.dot(med_ref[...], turn, preferred_element_type=f32)
    back_ref[...] = med_ref[...].astype(f32)
    loads[3].wait()
    loads[4].wait()
    loads[6].wait()
    if inline:

        def pick(peer):
            slot = jnp.int32(0)
            for i in range(per_device):
                slot = jnp.where(home[me * per_device + i] == peer, i, slot)
            return slot

        def origin_of(slot):
            source = jnp.int32(0)
            for i in range(n * per_device):
                hit = (home[i] == me) & (start[i] == slot * piece_rows)
                source = jnp.where(hit, i // per_device, source)
            return source

        origins = [origin_of(slot) for slot in range(per_device)]
    else:

        def pick(peer):
            return home[peer]

        origins = [start[slot] for slot in range(per_device)]

    up(rim_hop, False)

    def rim_step(q):
        cols = columns(q)
        found = []
        for k in range(3):
            wide_ref[k, 0:EDGE, cols] = rim_in[k, :, cols].astype(f32)
            found.append(stream(k, cols, GROUP))
            streams_ref[k, 0:GROUP, cols] = found[k]
        kv_ref[q, 0:GROUP] = (found[1] * found[2]).astype(kind)
        up(key_rest(q), True)

    chunks(0, nc, rim_step)
    owner = lax.broadcasted_iota(jnp.int32, (long_taps, chunk), 1) // GROUP
    flip = jnp.where(t + s == long_taps - 1, 1.0, 0.0).astype(kind)

    def banded(lines, q, window, near_mask):
        total = jnp.zeros((long_taps, chunk), f32)
        for g in range(near):
            line = jnp.broadcast_to(lines[pl.ds(q * near + g, 1), :], (long_taps, long_taps))
            wheel = pltpu.roll(line, 0, 1, stride=1, stride_axis=0)
            table = jnp.concatenate(
                [jnp.where(near_mask, wheel, 0.0), jnp.where(near_mask, 0.0, wheel)], axis=1
            ).astype(kind)
            product = jnp.dot(table, window, preferred_element_type=f32)
            total = jnp.where(owner == g, product, total)
        return total

    def send_step(q):
        cols = columns(q)
        pair(0, q).wait()
        total = mine_ref[0, :, cols].astype(f32) + got[0, q].astype(f32)
        for d in range(1, half):
            cross(d, q).wait()
            total = total + crossed[d, q].astype(f32)
        for i in range(per_device):
            pieces[q, i] = total[i * piece_rows : (i + 1) * piece_rows]

        def launch(k):
            stage[q, k] = pieces[q, pick(lax.rem(me + k, n))].astype(kind)
            route(q, k).start()

        peers(lambda j: launch(n - j))
        landed[q, 0] = pieces[q, pick(me)].astype(kind)

    def mixed_step(q):
        up(key_hop(q), False)
        up(key_rest(q), False)
        window = jnp.concatenate([key_in[q], kv_ref[q]], axis=0)
        ds_ref[0, 0:rows, columns(q)] = banded(filt_ref, q, window, s > t)

    chunks(0, nc, send_step)
    owned = lax.broadcasted_iota(jnp.int32, (width, long_taps), 0) // GROUP
    lane = lax.broadcasted_iota(jnp.int32, (width, long_taps), 1)
    member_ref[0] = jnp.where(owned == lane, 1.0, 0.0).astype(kind)
    member_ref[1] = jnp.where(owned + groups == lane, 1.0, 0.0).astype(kind)
    short_ref[...] = jnp.zeros_like(short_ref)
    last_ref[...] = jnp.zeros_like(last_ref)
    late_ref[...] = jnp.zeros_like(late_ref)
    ds_ref[:, rows:] = jnp.zeros((3, EDGE, width), f32)
    loads[5].wait()
    chunks(0, nc - 1, mixed_step)

    def short_sums(k, q, value):
        cols = columns(q)
        for lag in range(taps):
            short_ref[lag : lag + 1] = jnp.sum(
                value * wide_ref[k, EDGE - lag : EDGE - lag + rows, cols], axis=0, keepdims=True
            )
        exact = short_ref[...]
        high = exact.astype(kind)
        rest = exact - high.astype(f32)
        middle = rest.astype(kind)
        low = (rest - middle.astype(f32)).astype(kind)
        found = jnp.zeros((EDGE, long_taps), f32)
        for term in (high, middle, low):
            found = found + jnp.dot(
                term, member_ref[1 if k == 2 else 0, cols, :], preferred_element_type=f32
            )
        return found

    def receive(q):
        cols = columns(q)
        peers(lambda k: route(q, k).wait())
        ready[...] = landed[q]
        for slot in range(per_device):
            at = lax.rem(me - origins[slot] + n, n)
            acc[slot * piece_rows : (slot + 1) * piece_rows] = ready[at].astype(f32)
        acc[...] = out_grad_ref[:, cols].astype(f32) + acc[...]
        dmix_ref[q] = (acc[...] * streams_ref[0, :, cols]).astype(kind)
        down(mix_hop(q), True)

    def lag_step(q, lines):
        cols = columns(q)
        window = jnp.concatenate([key_in[q], kv_ref[q]], axis=0)
        flipped = jnp.dot(flip, dmix_ref[q], preferred_element_type=f32)
        for g in range(near):
            left = jnp.where(owner == g, flipped, 0.0).astype(kind)
            both = lax.dot_general(
                left, window, (((1,), (1,)), ((), ())), preferred_element_type=f32
            )
            ring = jnp.where(s + t <= long_taps - 1, both[:, long_taps:], both[:, :long_taps])
            ring = pltpu.roll(ring, 0, 1, stride=1, stride_axis=0)
            lines(g, jnp.sum(ring, axis=0, keepdims=True))
        value = acc[...] * ds_ref[0, 0:rows, cols]
        ds_ref[0, 0:rows, cols] = value
        last_ref[near : near + EDGE] = last_ref[near : near + EDGE] + short_sums(0, q, value)

    def early_lags(q):
        def lines(g, line):
            flat_ref[pl.ds(q * near + g, 1), :] = line

        lag_step(q, lines)

    def final_lines(g, line):
        last_ref[g : g + 1] = line

    def back_step(q):
        cols = columns(q)
        down(mix_hop(q), False)
        window = jnp.concatenate([dmix_ref[q], mix_in[q]], axis=0)
        total = banded(back_ref, q, window, s >= t)
        for k in (1, 2):
            value = total * streams_ref[3 - k, :, cols]
            ds_ref[k, 0:rows, cols] = value
            late_ref[...] = late_ref[...] + short_sums(k, q, value)
        head_ref[q] = ds_ref[:, 0:EDGE, cols].astype(kind)
        down(tail_hop(q), True)

    def feat_rows(k, q, low):
        cols = columns(q)
        total = wt_ref[k, 0:1, cols] * ds_ref[k, low:rows, cols]
        for lag in range(1, taps):
            total = total + wt_ref[k, lag : lag + 1, cols] * ds_ref[k, low + lag : rows + lag, cols]
        feat_out[k, low:, cols] = total.astype(feat_out.dtype)

    def feat_step(q):
        for k in range(3):
            feat_rows(k, q, 0)

    def tail_step(q):
        down(tail_hop(q), False)
        for k in range(3):
            ds_ref[k, rows:, columns(q)] = tail_in[q, k].astype(f32)
            feat_rows(k, q, rows - GROUP)

    share = part_ref.shape[1]
    used = (nc - 1) * near

    receive(0)
    early_lags(0)
    receive(1)
    mixed_step(nc - 1)
    early_lags(1)

    def both_steps(q):
        receive(q)
        back_step(q - 2)
        early_lags(q)

    chunks(2, nc - 1, both_steps)
    if n * share > used:
        flat_ref[used : n * share] = jnp.zeros((n * share - used, long_taps), f32)
    for k in range(n):
        part_ref[k] = flat_ref[k * share : (k + 1) * share]
    peers(lambda k: scatter(k).start())
    sums[0] = part_ref[me]
    receive(nc - 1)
    back_step(nc - 3)
    back_step(nc - 2)
    lag_step(nc - 1, final_lines)
    peers(lambda k: share_last(k).start())
    peers(lambda k: scatter(k).wait())
    result = sums[0]
    for k in range(1, n):
        result = result + sums[k]
    gathered[me] = result
    peers(lambda k: gather(k).start())
    back_step(nc - 1)
    peers(lambda k: share_late(k).start())
    chunks(0, nc, feat_step)
    chunks(0, nc, tail_step)
    peers(lambda k: gather(k).wait())
    for k in range(n):
        flat_ref[k * share : (k + 1) * share] = gathered[k]
    peers(lambda k: share_last(k).wait())
    total = last_ref[...]
    for k in range(1, n):
        total = total + last_in[k]
    flat_ref[used:groups] = total[0:near]
    mirror = jnp.where(t + s == long_taps - 1, 1.0, 0.0)
    med_out[...] = factor * jnp.dot(
        flat_ref[0:groups], mirror, precision=lax.Precision.HIGHEST, preferred_element_type=f32
    )
    peers(lambda k: share_late(k).wait())
    late = late_ref[...]
    for k in range(1, n):
        late = late + late_in[k]
    short_out[0] = factor * total[near : near + taps, :groups]
    short_out[1] = factor * late[:taps, :groups]
    short_out[2] = factor * late[:taps, groups : 2 * groups]


def store_kernel(feat_ref, short_ref, med_ref, feat_out, short_out, med_out, sems):
    copies = [
        pltpu.make_async_copy(source, target, sems.at[i])
        for i, (source, target) in enumerate(
            [(feat_ref, feat_out), (short_ref, short_out), (med_ref, med_out)]
        )
    ]
    for copy in copies:
        copy.start()
    for copy in copies:
        copy.wait()


def tables(piece_home, piece_start, ctx_count, per_device, piece_rows):
    own_index = lax.axis_index("ctx")
    everyone = piece_home.reshape(ctx_count, per_device)
    positions = (piece_start // piece_rows).reshape(ctx_count, per_device)
    local_home = lax.dynamic_slice_in_dim(everyone, own_index, 1, 0)[0]
    device_ids = jnp.arange(ctx_count, dtype=jnp.int32)
    slot_ids = jnp.arange(per_device, dtype=jnp.int32)
    matches = local_home[None, :] == device_ids[:, None]
    send_slot = jnp.sum(jnp.where(matches, slot_ids[None, :], 0), axis=1)
    keyed = jnp.where(everyone == own_index, positions, -1)
    hits = jnp.any(keyed[:, :, None] == slot_ids[None, None, :], axis=1)
    source_of = jnp.sum(jnp.where(hits, device_ids[:, None], 0), axis=0)
    return send_slot.astype(jnp.int32), source_of.astype(jnp.int32)


def shards(features, out_grad, attn_parts, short_filt, med_filt, piece_home, piece_start):
    rows, width = out_grad.shape
    groups, taps = med_filt.shape
    short_taps = short_filt.shape[2]
    ctx_count = lax.axis_size("ctx")
    tp_count = lax.axis_size("tp")
    per_device = ctx_count // 2
    piece_rows = rows // per_device
    factor = 1.0 / math.sqrt(rows * ctx_count * GROUP)
    chunk = LANES
    nc = width // chunk
    near = chunk // GROUP
    f32, half = jnp.float32, features.dtype
    inline = ctx_count * per_device <= 64
    if inline:
        home, start = piece_home, piece_start
    else:
        home, start = tables(piece_home, piece_start, ctx_count, per_device, piece_rows)

    vmem = pl.BlockSpec(memory_space=pltpu.VMEM)
    hbm = pl.BlockSpec(memory_space=pltpu.HBM)
    dma = pltpu.SemaphoreType.DMA
    share = -(-((nc - 1) * near) // ctx_count)
    parts = pltpu.VMEM((ctx_count, share, taps), f32)
    held = pltpu.VMEM((nc, rows, chunk), half)
    wide = pltpu.VMEM((3, rows, width), f32)
    padded = pltpu.VMEM((3, rows + EDGE, width), f32)
    crossing = pltpu.VMEM((tp_count // 2, nc, rows, chunk), half)
    routed = pltpu.VMEM((nc, ctx_count, piece_rows, chunk), half)
    heads = pltpu.VMEM((nc, 3, EDGE, chunk), half)
    flags = dma((tp_count // 2, nc))
    lanes = dma((nc, ctx_count))
    peers = dma((ctx_count,))
    outs = (
        jax.ShapeDtypeStruct((3, rows, width), half),
        jax.ShapeDtypeStruct((3, short_taps, groups), f32),
        jax.ShapeDtypeStruct((groups, taps), f32),
    )
    found = pl.pallas_call(
        functools.partial(whole_kernel, ctx_count, tp_count, inline, factor),
        in_specs=[hbm] * 7,
        out_specs=(vmem,) * 3,
        out_shape=outs,
        scratch_shapes=[
            pltpu.SMEM(home.shape, jnp.int32), pltpu.SMEM(start.shape, jnp.int32),
            pltpu.VMEM((3, rows, width), half), pltpu.VMEM((rows, width), half),
            pltpu.VMEM((tp_count // 2, rows, width), half),
            pltpu.VMEM((3, short_taps, groups), half), pltpu.VMEM((groups, taps), half),
            pltpu.VMEM((3, 8, width), f32), pltpu.VMEM((groups, taps), f32),
            pltpu.VMEM((groups, taps), f32), pltpu.VMEM((2, width, taps), half),
            padded, pltpu.VMEM((EDGE, chunk), f32),
            wide, held, held, padded,
            pltpu.VMEM((rows, chunk), f32),
            crossing, crossing, crossing,
            pltpu.VMEM((nc, per_device, piece_rows, chunk), f32), routed, routed,
            pltpu.VMEM((ctx_count, piece_rows, chunk), half),
            pltpu.VMEM((3, EDGE, width), half), held, held, heads, heads,
            pltpu.VMEM((max(groups, ctx_count * share), taps), f32), parts, parts, parts,
            pltpu.VMEM((near + EDGE, taps), f32), pltpu.VMEM((ctx_count, near + EDGE, taps), f32),
            pltpu.VMEM((EDGE, taps), f32), pltpu.VMEM((ctx_count, EDGE, taps), f32),
            dma((6 + tp_count // 2,)), flags, flags, flags, flags, lanes, lanes,
            dma((2,)), dma((4, nc)), dma((4, nc)),
            peers, peers, peers, peers, peers, peers, peers, peers,
        ],
        compiler_params=pltpu.CompilerParams(
            collective_id=0, has_side_effects=True, vmem_limit_bytes=36 * 1024 * 1024
        ),
        cost_estimate=cost(12 * groups * taps * taps * chunk, 40 * rows * width),
    )(
        *[
            pltpu.with_memory_space_constraint(x, pltpu.HBM)
            for x in (
                home, start, attn_parts[0], features, out_grad,
                jnp.transpose(short_filt, (0, 2, 1)), med_filt,
            )
        ]
    )
    feat_grad, short_grad, med_grad = pl.pallas_call(
        store_kernel,
        in_specs=[vmem] * 3,
        out_specs=(hbm,) * 3,
        out_shape=outs,
        scratch_shapes=[dma((3,))],
        compiler_params=pltpu.CompilerParams(vmem_limit_bytes=4 * 1024 * 1024),
        cost_estimate=cost(0, 8 * rows * width),
    )(*found)
    return feat_grad, jnp.transpose(short_grad, (0, 2, 1)), med_grad


def solution(mesh):
    return jax.shard_map(
        shards,
        mesh=mesh,
        in_specs=(
            P(None, "ctx", "tp"),
            P("ctx", "tp"),
            P("tp", "ctx", None),
            P(None, "tp", None),
            P("tp", None),
            P(),
            P(),
        ),
        out_specs=(P(None, "ctx", "tp"), P(None, "tp", None), P("tp", None)),
        check_vma=False,
    )
```

```python
import functools
import math

import jax
import jax.numpy as jnp
from jax import lax
from jax.experimental import pallas as pl
from jax.experimental.pallas import tpu as pltpu
from jax.sharding import PartitionSpec as P

GROUP = 16
MESH = pl.DeviceIdType.MESH
LANES = 256
EDGE = 8


def cost(flops, bytes_accessed):
    return pl.CostEstimate(flops=flops, bytes_accessed=bytes_accessed, transcendentals=0)


def plane(rows, axis):
    return lax.broadcasted_iota(jnp.int32, (rows, rows), axis)


def whole_kernel(
    n, tp, inline, factor,
    home_hbm, start_hbm, attn_hbm, feat_hbm, grad_hbm, taps_hbm, med_hbm,
    feat_out, short_out, med_out,
    home, start, feat_ref, out_grad_ref, mine_ref, taps_ref, med_ref,
    wt_ref, filt_ref, back_ref, member_ref, wide_ref, short_ref,
    streams_ref, kv_ref, dmix_ref, ds_ref, acc,
    got, passed, crossed, pieces, stage, landed, ready,
    rim_in, key_in, mix_in, head_ref, tail_in,
    flat_ref, part_ref, sums, gathered, last_ref, last_in, late_ref, late_in,
    local, pair_send, pair_recv, cross_send, cross_recv, send, recv, rim_sems, halo_send, halo_recv,
    send1, recv1, send2, recv2, send3, recv3, send4, recv4,
):
    me = lax.axis_index("ctx")
    col = lax.axis_index("tp")
    f32 = jnp.float32
    nc, rows, chunk = kv_ref.shape
    width = nc * chunk
    taps = taps_ref.shape[1]
    groups, long_taps = med_ref.shape
    per_device, piece_rows = pieces.shape[1:3]
    near = chunk // GROUP
    half = tp // 2
    side, row = lax.rem(col, 2), col // 2
    partner = row * 2 + 1 - side
    kind = kv_ref.dtype
    barrier = pltpu.get_barrier_semaphore()

    def other(d):
        return lax.rem(row + d, half) * 2 + side

    def peers(act):
        def step(k, carry):
            act(k)
            return carry

        lax.fori_loop(1, n, step, 0, unroll=inline)

    def greet(k):
        pl.semaphore_signal(
            barrier, inc=1, device_id={"ctx": lax.rem(me + k, n)}, device_id_type=MESH
        )

    peers(greet)
    pl.semaphore_signal(barrier, inc=1, device_id={"tp": partner}, device_id_type=MESH)
    for d in range(1, half):
        pl.semaphore_signal(barrier, inc=1, device_id={"tp": other(d)}, device_id_type=MESH)

    def slab(which):
        return pl.ds(pl.multiple_of(which * width, width), width)

    def part(which, q):
        return pl.ds(pl.multiple_of(which * width + q * chunk, chunk), chunk)

    def load(source, target, at):
        return pltpu.make_async_copy(source, target, local.at[at])

    loads = [
        load(taps_hbm, taps_ref, 0), load(med_hbm, med_ref, 1), load(feat_hbm, feat_ref, 2),
        load(home_hbm, home, 3), load(start_hbm, start, 4), load(grad_hbm, out_grad_ref, 5),
    ] + [
        load(attn_hbm.at[:, slab(other(d))], mine_ref.at[d], 6 + d) for d in range(half)
    ]
    for at in [6 + d for d in range(1, half)] + [0, 2]:
        loads[at].start()

    def hop(source, target, by, sends, recvs):
        return pltpu.make_async_remote_copy(
            source, target, sends, recvs,
            device_id={"ctx": lax.rem(me + by + n, n)}, device_id_type=MESH,
        )

    def up(copy, begin):
        if begin:
            pl.when(me < n - 1)(copy.start)
        else:
            pl.when(me < n - 1)(copy.wait_send)
            pl.when(me > 0)(copy.wait_recv)

    def down(copy, begin):
        if begin:
            pl.when(me > 0)(copy.start)
        else:
            pl.when(me > 0)(copy.wait_send)
            pl.when(me < n - 1)(copy.wait_recv)

    def key_hop(q):
        body = pl.ds(GROUP, rows - GROUP)
        return hop(
            kv_ref.at[q, body], key_in.at[q, body], 1, halo_send.at[0, q], halo_recv.at[0, q]
        )

    def key_rest(q):
        body = pl.ds(0, GROUP)
        return hop(
            kv_ref.at[q, body], key_in.at[q, body], 1, halo_send.at[3, q], halo_recv.at[3, q]
        )

    def mix_hop(q):
        return hop(dmix_ref.at[q], mix_in.at[q], -1, halo_send.at[1, q], halo_recv.at[1, q])

    def tail_hop(q):
        return hop(head_ref.at[q], tail_in.at[q], -1, halo_send.at[2, q], halo_recv.at[2, q])

    def pair(d, q):
        line = lax.rem(row + d, half)
        return pltpu.make_async_remote_copy(
            attn_hbm.at[:, part(line * 2 + 1 - side, q)], got.at[d, q],
            pair_send.at[d, q], pair_recv.at[d, q],
            device_id={"tp": partner}, device_id_type=MESH,
        )

    def cross(d, q):
        return pltpu.make_async_remote_copy(
            passed.at[d, q], crossed.at[d, q], cross_send.at[d, q], cross_recv.at[d, q],
            device_id={"tp": other(d)}, device_id_type=MESH,
        )

    def route(q, k):
        return pltpu.make_async_remote_copy(
            stage.at[q, k], landed.at[q, k], send.at[q, k], recv.at[q, k],
            device_id={"ctx": lax.rem(me + k, n)}, device_id_type=MESH,
        )

    def scatter(k):
        peer = lax.rem(me + k, n)
        return pltpu.make_async_remote_copy(
            part_ref.at[peer], sums.at[k], send1.at[k], recv1.at[k],
            device_id={"ctx": peer}, device_id_type=MESH,
        )

    def gather(k):
        return pltpu.make_async_remote_copy(
            gathered.at[me], gathered.at[me], send2.at[k], recv2.at[k],
            device_id={"ctx": lax.rem(me + k, n)}, device_id_type=MESH,
        )

    def share_last(k):
        return pltpu.make_async_remote_copy(
            last_ref, last_in.at[k], send3.at[k], recv3.at[k],
            device_id={"ctx": lax.rem(me + k, n)}, device_id_type=MESH,
        )

    def share_late(k):
        return pltpu.make_async_remote_copy(
            late_ref, late_in.at[k], send4.at[k], recv4.at[k],
            device_id={"ctx": lax.rem(me + k, n)}, device_id_type=MESH,
        )

    def columns(q):
        return pl.ds(pl.multiple_of(q * chunk, chunk), chunk)

    def chunks(low, high, act):
        def step(q, carry):
            act(q)
            return carry

        lax.fori_loop(low, high, step, 0)

    @pl.when(me == 0)
    def clear_first():
        rim_in[...] = jnp.zeros_like(rim_in)
        key_in[...] = jnp.zeros_like(key_in)

    @pl.when(me == n - 1)
    def clear_last():
        mix_in[...] = jnp.zeros_like(mix_in)
        tail_in[...] = jnp.zeros_like(tail_in)

    pl.semaphore_wait(barrier, n - 1 + half)
    rim_hop = hop(
        feat_hbm.at[:, pl.ds(rows - EDGE, EDGE), :], rim_in, 1, rim_sems.at[0], rim_sems.at[1]
    )
    up(rim_hop, True)
    for d in [d for d in range(1, half)] + [0]:
        chunks(0, nc, lambda q, d=d: pair(d, q).start())
    for at in (1, 6, 3, 4, 5):
        loads[at].start()

    wide_ref[:, 0:EDGE] = jnp.zeros((3, EDGE, width), f32)
    loads[0].wait()
    spread = jnp.where(
        lax.broadcasted_iota(jnp.int32, (groups, width), 0)
        == lax.broadcasted_iota(jnp.int32, (groups, width), 1) // GROUP,
        1.0,
        0.0,
    ).astype(kind)
    for s in range(3):
        wt_ref[s, 0:taps] = jnp.dot(taps_ref[s], spread, preferred_element_type=f32)
    loads[2].wait()

    def stream(k, cols, count):
        total = wt_ref[k, 0:1, cols] * wide_ref[k, EDGE : EDGE + count, cols]
        for lag in range(1, taps):
            rows_back = wide_ref[k, EDGE - lag : EDGE - lag + count, cols]
            total = total + wt_ref[k, lag : lag + 1, cols] * rows_back
        return total

    def stream_step(q):
        cols = columns(q)
        found = []
        for k in range(3):
            wide_ref[k, EDGE : EDGE + rows, cols] = feat_ref[k, :, cols].astype(f32)
            found.append(stream(k, cols, rows))
            streams_ref[k, :, cols] = found[k]
        kv_ref[q, GROUP:] = (found[1] * found[2])[GROUP:].astype(kind)
        up(key_hop(q), True)
        for d in range(1, half):
            pair(d, q).wait()
            passed[d, q] = (mine_ref[d, :, cols].astype(f32) + got[d, q].astype(f32)).astype(kind)
            cross(d, q).start()

    for d in range(1, half):
        loads[6 + d].wait()
    chunks(0, nc, stream_step)
    t, s = plane(long_taps, 0), plane(long_taps, 1)
    loads[1].wait()
    turn = jnp.where((t + s == 0) | (t + s == long_taps), 1.0, 0.0).astype(kind)
    filt_ref[...] = jnp.dot(med_ref[...], turn, preferred_element_type=f32)
    back_ref[...] = med_ref[...].astype(f32)
    loads[3].wait()
    loads[4].wait()
    loads[6].wait()
    if inline:

        def pick(peer):
            slot = jnp.int32(0)
            for i in range(per_device):
                slot = jnp.where(home[me * per_device + i] == peer, i, slot)
            return slot

        def origin_of(slot):
            source = jnp.int32(0)
            for i in range(n * per_device):
                hit = (home[i] == me) & (start[i] == slot * piece_rows)
                source = jnp.where(hit, i // per_device, source)
            return source

        origins = [origin_of(slot) for slot in range(per_device)]
    else:

        def pick(peer):
            return home[peer]

        origins = [start[slot] for slot in range(per_device)]

    up(rim_hop, False)

    def rim_step(q):
        cols = columns(q)
        found = []
        for k in range(3):
            wide_ref[k, 0:EDGE, cols] = rim_in[k, :, cols].astype(f32)
            found.append(stream(k, cols, GROUP))
            streams_ref[k, 0:GROUP, cols] = found[k]
        kv_ref[q, 0:GROUP] = (found[1] * found[2]).astype(kind)
        up(key_rest(q), True)

    chunks(0, nc, rim_step)
    owner = lax.broadcasted_iota(jnp.int32, (long_taps, chunk), 1) // GROUP
    flip = jnp.where(t + s == long_taps - 1, 1.0, 0.0).astype(kind)

    def banded(lines, q, window, near_mask):
        total = jnp.zeros((long_taps, chunk), f32)
        for g in range(near):
            line = jnp.broadcast_to(lines[pl.ds(q * near + g, 1), :], (long_taps, long_taps))
            wheel = pltpu.roll(line, 0, 1, stride=1, stride_axis=0)
            table = jnp.concatenate(
                [jnp.where(near_mask, wheel, 0.0), jnp.where(near_mask, 0.0, wheel)], axis=1
            ).astype(kind)
            product = jnp.dot(table, window, preferred_element_type=f32)
            total = jnp.where(owner == g, product, total)
        return total

    def send_step(q):
        cols = columns(q)
        pair(0, q).wait()
        total = mine_ref[0, :, cols].astype(f32) + got[0, q].astype(f32)
        for d in range(1, half):
            cross(d, q).wait()
            total = total + crossed[d, q].astype(f32)
        for i in range(per_device):
            pieces[q, i] = total[i * piece_rows : (i + 1) * piece_rows]

        def launch(k):
            stage[q, k] = pieces[q, pick(lax.rem(me + k, n))].astype(kind)
            route(q, k).start()

        peers(lambda j: launch(n - j))
        landed[q, 0] = pieces[q, pick(me)].astype(kind)

    def mixed_step(q):
        up(key_hop(q), False)
        up(key_rest(q), False)
        window = jnp.concatenate([key_in[q], kv_ref[q]], axis=0)
        ds_ref[0, 0:rows, columns(q)] = banded(filt_ref, q, window, s > t)

    chunks(0, nc, send_step)
    owned = lax.broadcasted_iota(jnp.int32, (width, long_taps), 0) // GROUP
    lane = lax.broadcasted_iota(jnp.int32, (width, long_taps), 1)
    member_ref[0] = jnp.where(owned == lane, 1.0, 0.0).astype(kind)
    member_ref[1] = jnp.where(owned + groups == lane, 1.0, 0.0).astype(kind)
    short_ref[...] = jnp.zeros_like(short_ref)
    last_ref[...] = jnp.zeros_like(last_ref)
    late_ref[...] = jnp.zeros_like(late_ref)
    ds_ref[:, rows:] = jnp.zeros((3, EDGE, width), f32)
    loads[5].wait()
    chunks(0, nc - 1, mixed_step)

    def short_sums(k, q, value):
        cols = columns(q)
        for lag in range(taps):
            short_ref[lag : lag + 1] = jnp.sum(
                value * wide_ref[k, EDGE - lag : EDGE - lag + rows, cols], axis=0, keepdims=True
            )
        exact = short_ref[...]
        high = exact.astype(kind)
        rest = exact - high.astype(f32)
        middle = rest.astype(kind)
        low = (rest - middle.astype(f32)).astype(kind)
        found = jnp.zeros((EDGE, long_taps), f32)
        for term in (high, middle, low):
            found = found + jnp.dot(
                term, member_ref[1 if k == 2 else 0, cols, :], preferred_element_type=f32
            )
        return found

    def receive(q):
        cols = columns(q)
        peers(lambda k: route(q, k).wait())
        ready[...] = landed[q]
        for slot in range(per_device):
            at = lax.rem(me - origins[slot] + n, n)
            acc[slot * piece_rows : (slot + 1) * piece_rows] = ready[at].astype(f32)
        acc[...] = out_grad_ref[:, cols].astype(f32) + acc[...]
        dmix_ref[q] = (acc[...] * streams_ref[0, :, cols]).astype(kind)
        down(mix_hop(q), True)

    def lag_step(q, lines):
        cols = columns(q)
        window = jnp.concatenate([key_in[q], kv_ref[q]], axis=0)
        flipped = jnp.dot(flip, dmix_ref[q], preferred_element_type=f32)
        for g in range(near):
            left = jnp.where(owner == g, flipped, 0.0).astype(kind)
            both = lax.dot_general(
                left, window, (((1,), (1,)), ((), ())), preferred_element_type=f32
            )
            ring = jnp.where(s + t <= long_taps - 1, both[:, long_taps:], both[:, :long_taps])
            ring = pltpu.roll(ring, 0, 1, stride=1, stride_axis=0)
            lines(g, jnp.sum(ring, axis=0, keepdims=True))
        value = acc[...] * ds_ref[0, 0:rows, cols]
        ds_ref[0, 0:rows, cols] = value
        last_ref[near : near + EDGE] = last_ref[near : near + EDGE] + short_sums(0, q, value)

    def early_lags(q):
        def lines(g, line):
            flat_ref[pl.ds(q * near + g, 1), :] = line

        lag_step(q, lines)

    def final_lines(g, line):
        last_ref[g : g + 1] = line

    def back_step(q, final=False):
        cols = columns(q)
        down(mix_hop(q), False)
        window = jnp.concatenate([dmix_ref[q], mix_in[q]], axis=0)
        total = banded(back_ref, q, window, s >= t)
        for k in (1, 2):
            value = total * streams_ref[3 - k, :, cols]
            ds_ref[k, 0:rows, cols] = value
            late_ref[...] = late_ref[...] + short_sums(k, q, value)
        if final:
            peers(lambda k: share_late(k).start())
        head_ref[q] = ds_ref[:, 0:EDGE, cols].astype(kind)
        down(tail_hop(q), True)

    def feat_rows(k, q, low):
        cols = columns(q)
        total = wt_ref[k, 0:1, cols] * ds_ref[k, low:rows, cols]
        for lag in range(1, taps):
            total = total + wt_ref[k, lag : lag + 1, cols] * ds_ref[k, low + lag : rows + lag, cols]
        feat_out[k, low:, cols] = total.astype(feat_out.dtype)

    def feat_step(q):
        for k in range(3):
            feat_rows(k, q, 0)

    def tail_step(q):
        down(tail_hop(q), False)
        for k in range(3):
            ds_ref[k, rows:, columns(q)] = tail_in[q, k].astype(f32)
            feat_rows(k, q, rows - GROUP)

    share = part_ref.shape[1]
    used = (nc - 1) * near

    receive(0)
    early_lags(0)
    receive(1)
    mixed_step(nc - 1)
    early_lags(1)

    def both_steps(q):
        receive(q)
        back_step(q - 2)
        early_lags(q)

    chunks(2, nc - 1, both_steps)
    if n * share > used:
        flat_ref[used : n * share] = jnp.zeros((n * share - used, long_taps), f32)
    for k in range(n):
        part_ref[k] = flat_ref[k * share : (k + 1) * share]
    peers(lambda k: scatter(k).start())
    sums[0] = part_ref[me]
    receive(nc - 1)
    back_step(nc - 3)
    back_step(nc - 2)
    lag_step(nc - 1, final_lines)
    peers(lambda k: share_last(k).start())
    peers(lambda k: scatter(k).wait())
    result = sums[0]
    for k in range(1, n):
        result = result + sums[k]
    gathered[me] = result
    peers(lambda k: gather(k).start())
    back_step(nc - 1, final=True)
    chunks(0, nc, feat_step)
    chunks(0, nc, tail_step)
    peers(lambda k: gather(k).wait())
    for k in range(n):
        flat_ref[k * share : (k + 1) * share] = gathered[k]
    peers(lambda k: share_last(k).wait())
    total = last_ref[...]
    for k in range(1, n):
        total = total + last_in[k]
    flat_ref[used:groups] = total[0:near]
    mirror = jnp.where(t + s == long_taps - 1, 1.0, 0.0)
    med_out[...] = factor * jnp.dot(
        flat_ref[0:groups], mirror, precision=lax.Precision.HIGHEST, preferred_element_type=f32
    )
    peers(lambda k: share_late(k).wait())
    late = late_ref[...]
    for k in range(1, n):
        late = late + late_in[k]
    short_out[0] = factor * total[near : near + taps, :groups]
    short_out[1] = factor * late[:taps, :groups]
    short_out[2] = factor * late[:taps, groups : 2 * groups]


def store_kernel(feat_ref, short_ref, med_ref, feat_out, short_out, med_out, sems):
    copies = [
        pltpu.make_async_copy(source, target, sems.at[i])
        for i, (source, target) in enumerate(
            [(feat_ref, feat_out), (short_ref, short_out), (med_ref, med_out)]
        )
    ]
    for copy in copies:
        copy.start()
    for copy in copies:
        copy.wait()


def tables(piece_home, piece_start, ctx_count, per_device, piece_rows):
    own_index = lax.axis_index("ctx")
    everyone = piece_home.reshape(ctx_count, per_device)
    positions = (piece_start // piece_rows).reshape(ctx_count, per_device)
    local_home = lax.dynamic_slice_in_dim(everyone, own_index, 1, 0)[0]
    device_ids = jnp.arange(ctx_count, dtype=jnp.int32)
    slot_ids = jnp.arange(per_device, dtype=jnp.int32)
    matches = local_home[None, :] == device_ids[:, None]
    send_slot = jnp.sum(jnp.where(matches, slot_ids[None, :], 0), axis=1)
    keyed = jnp.where(everyone == own_index, positions, -1)
    hits = jnp.any(keyed[:, :, None] == slot_ids[None, None, :], axis=1)
    source_of = jnp.sum(jnp.where(hits, device_ids[:, None], 0), axis=0)
    return send_slot.astype(jnp.int32), source_of.astype(jnp.int32)


def shards(features, out_grad, attn_parts, short_filt, med_filt, piece_home, piece_start):
    rows, width = out_grad.shape
    groups, taps = med_filt.shape
    short_taps = short_filt.shape[2]
    ctx_count = lax.axis_size("ctx")
    tp_count = lax.axis_size("tp")
    per_device = ctx_count // 2
    piece_rows = rows // per_device
    factor = 1.0 / math.sqrt(rows * ctx_count * GROUP)
    chunk = LANES
    nc = width // chunk
    near = chunk // GROUP
    f32, half = jnp.float32, features.dtype
    inline = ctx_count * per_device <= 64
    if inline:
        home, start = piece_home, piece_start
    else:
        home, start = tables(piece_home, piece_start, ctx_count, per_device, piece_rows)

    vmem = pl.BlockSpec(memory_space=pltpu.VMEM)
    hbm = pl.BlockSpec(memory_space=pltpu.HBM)
    dma = pltpu.SemaphoreType.DMA
    share = -(-((nc - 1) * near) // ctx_count)
    parts = pltpu.VMEM((ctx_count, share, taps), f32)
    held = pltpu.VMEM((nc, rows, chunk), half)
    wide = pltpu.VMEM((3, rows, width), f32)
    padded = pltpu.VMEM((3, rows + EDGE, width), f32)
    crossing = pltpu.VMEM((tp_count // 2, nc, rows, chunk), half)
    routed = pltpu.VMEM((nc, ctx_count, piece_rows, chunk), half)
    heads = pltpu.VMEM((nc, 3, EDGE, chunk), half)
    flags = dma((tp_count // 2, nc))
    lanes = dma((nc, ctx_count))
    peers = dma((ctx_count,))
    outs = (
        jax.ShapeDtypeStruct((3, rows, width), half),
        jax.ShapeDtypeStruct((3, short_taps, groups), f32),
        jax.ShapeDtypeStruct((groups, taps), f32),
    )
    found = pl.pallas_call(
        functools.partial(whole_kernel, ctx_count, tp_count, inline, factor),
        in_specs=[hbm] * 7,
        out_specs=(vmem,) * 3,
        out_shape=outs,
        scratch_shapes=[
            pltpu.SMEM(home.shape, jnp.int32), pltpu.SMEM(start.shape, jnp.int32),
            pltpu.VMEM((3, rows, width), half), pltpu.VMEM((rows, width), half),
            pltpu.VMEM((tp_count // 2, rows, width), half),
            pltpu.VMEM((3, short_taps, groups), half), pltpu.VMEM((groups, taps), half),
            pltpu.VMEM((3, 8, width), f32), pltpu.VMEM((groups, taps), f32),
            pltpu.VMEM((groups, taps), f32), pltpu.VMEM((2, width, taps), half),
            padded, pltpu.VMEM((EDGE, chunk), f32),
            wide, held, held, padded,
            pltpu.VMEM((rows, chunk), f32),
            crossing, crossing, crossing,
            pltpu.VMEM((nc, per_device, piece_rows, chunk), f32), routed, routed,
            pltpu.VMEM((ctx_count, piece_rows, chunk), half),
            pltpu.VMEM((3, EDGE, width), half), held, held, heads, heads,
            pltpu.VMEM((max(groups, ctx_count * share), taps), f32), parts, parts, parts,
            pltpu.VMEM((near + EDGE, taps), f32), pltpu.VMEM((ctx_count, near + EDGE, taps), f32),
            pltpu.VMEM((EDGE, taps), f32), pltpu.VMEM((ctx_count, EDGE, taps), f32),
            dma((6 + tp_count // 2,)), flags, flags, flags, flags, lanes, lanes,
            dma((2,)), dma((4, nc)), dma((4, nc)),
            peers, peers, peers, peers, peers, peers, peers, peers,
        ],
        compiler_params=pltpu.CompilerParams(
            collective_id=0, has_side_effects=True, vmem_limit_bytes=36 * 1024 * 1024
        ),
        cost_estimate=cost(12 * groups * taps * taps * chunk, 40 * rows * width),
    )(
        *[
            pltpu.with_memory_space_constraint(x, pltpu.HBM)
            for x in (
                home, start, attn_parts[0], features, out_grad,
                jnp.transpose(short_filt, (0, 2, 1)), med_filt,
            )
        ]
    )
    feat_grad, short_grad, med_grad = pl.pallas_call(
        store_kernel,
        in_specs=[vmem] * 3,
        out_specs=(hbm,) * 3,
        out_shape=outs,
        scratch_shapes=[dma((3,))],
        compiler_params=pltpu.CompilerParams(vmem_limit_bytes=4 * 1024 * 1024),
        cost_estimate=cost(0, 8 * rows * width),
    )(*found)
    return feat_grad, jnp.transpose(short_grad, (0, 2, 1)), med_grad


def solution(mesh):
    return jax.shard_map(
        shards,
        mesh=mesh,
        in_specs=(
            P(None, "ctx", "tp"),
            P("ctx", "tp"),
            P("tp", "ctx", None),
            P(None, "tp", None),
            P("tp", None),
            P(),
            P(),
        ),
        out_specs=(P(None, "ctx", "tp"), P(None, "tp", None), P("tp", None)),
        check_vma=False,
    )
```
